32 devices in a mesh: row: 8 (over z, core), col: 4 (over y, x).
Axes of the slice: x: 2, y: 2, z: 4, core: 2. Of those that a mesh axis runs over, the one named last changes fastest.
Arguments:
- affinity: float32 [16384, 16384], P('row', 'col'), as said below
Outputs:
- reduced: float32 [16384, 16384], P('row', 'col')
Inputs may be any that keep to these rules, and one draw needn't show every extreme that they name: The matrix that affinity stores is exactly symmetric in global indexing.
All inputs are finite; a program needn't handle non-finite values.
Results may differ from the reference program's by a relative error of at most 0.0003.
Values sent between devices are 32-bit elements; how exact they have to be, the bound alone decides.
No kernel may reach another device: no remote copies, remote signals or barrier semaphores. Data moves between devices by JAX's collectives and lax.ppermute only.
A program may use at most 192 MiB of HBM per device.

```python
import math
import jax
import jax.numpy as jnp
from jax import lax

N = 16384
B = 256
PANELS = 2
NS_STEPS = 12
ROW_BLOCKS = 8
COL_BLOCKS = 16
N_ROW = 8
N_COL = 4


def draw_affinity(key, part):
    noise_key = jax.random.fold_in(key, 11)
    scale_key = jax.random.fold_in(key, 12)
    uniform_noise = jax.random.uniform(noise_key, (N, N), jnp.float32, -1.0, 1.0)
    sym_part = 0.5 * (uniform_noise + uniform_noise.T)
    scales = jnp.exp(jax.random.uniform(scale_key, (N,), jnp.float32, 0.0, math.log(10.0)))
    dense_matrix = 0.25 * sym_part * (scales[:, None] * scales[None, :])
    lower_index = jnp.arange(N - B, dtype=jnp.int32)
    upper_index = lower_index + B
    band_value = 64.0 * (scales[upper_index] * scales[lower_index])
    dense_matrix = dense_matrix.at[upper_index, lower_index].add(band_value)
    dense_matrix = dense_matrix.at[lower_index, upper_index].add(band_value)
    row_devices = N // (B * ROW_BLOCKS)
    col_devices = N // (B * COL_BLOCKS)
    rows_here = N // row_devices
    cols_here = N // col_devices
    stored_index = jnp.arange(N, dtype=jnp.int32)
    row_order = (stored_index % rows_here // B * row_devices + stored_index // rows_here) * B + stored_index % B
    col_order = (stored_index % cols_here // B * col_devices + stored_index // cols_here) * B + stored_index % B
    return jnp.take(jnp.take(dense_matrix, row_order, axis=0), col_order, axis=1)


def setup_inputs(seed: int = 0) -> dict:
    key_of = jax.random.split(jax.random.key(seed), 2)
    return {
        "affinity": draw_affinity(jax.random.fold_in(key_of[1], 71), 0),
    }


PRECISE = lax.Precision.HIGHEST

def matmul(first_op, second_op, first_dim, second_dim):
    return lax.dot_general(first_op.astype(jnp.float32), second_op.astype(jnp.float32), (((first_dim,), (second_dim,)), ((), ())), precision=PRECISE, preferred_element_type=jnp.float32)

def lower_inverse(square):
    lower_factor = jnp.linalg.cholesky(square)
    identity = jnp.eye(square.shape[0], dtype=jnp.float32)
    return lax.linalg.triangular_solve(lower_factor, identity, left_side=True, lower=True)

def reflector_parts(gram_matrix, top_block):
    inverse_low = lower_inverse(gram_matrix)
    top_basis = matmul(top_block, inverse_low, 1, 1)
    polar_part = top_basis
    for repeat in range(NS_STEPS):
        polar_part = 1.5 * polar_part - 0.5 * matmul(polar_part, matmul(polar_part, polar_part, 0, 0), 1, 0)
    cross_term = matmul(polar_part, top_basis, 0, 0)
    identity = jnp.eye(gram_matrix.shape[0], dtype=jnp.float32)
    metric = identity + cross_term + cross_term.T + matmul(polar_part, polar_part, 0, 0)
    metric_inv = lower_inverse(metric)
    middle = 2.0 * matmul(metric_inv, metric_inv, 0, 0)
    return (inverse_low, polar_part, middle)

def reference(affinity):
    rows_here = N // N_ROW
    cols_here = N // N_COL
    stored = jnp.arange(N, dtype=jnp.int32)
    row_blocks = stored % rows_here // B * N_ROW + stored // rows_here
    col_device = stored // cols_here
    col_global = stored % cols_here // B * N_COL + col_device
    col_within = stored % B
    row_place = (col_global % N_ROW * rows_here + col_global // N_ROW * B + col_within).astype(jnp.int32)
    matrix = affinity
    for panel_num in range(PANELS):
        col_start = panel_num % N_COL * cols_here + panel_num // N_COL * B
        panel_rows = jnp.where((row_blocks > panel_num)[:, None], matrix[:, col_start:col_start + B], 0.0)
        top_start = (panel_num + 1) % N_ROW * rows_here + (panel_num + 1) // N_ROW * B
        gram_matrix = matmul(panel_rows, panel_rows, 0, 0)
        inverse_low, polar_part, middle = reflector_parts(gram_matrix, panel_rows[top_start:top_start + B])
        reflect_rows = matmul(panel_rows, inverse_low, 1, 1).at[top_start:top_start + B].add(polar_part)
        reflect_cols = jnp.take(reflect_rows, row_place, axis=0)
        product_rows = matmul(matrix, reflect_cols, 1, 0)
        image_rows = matmul(product_rows, middle, 1, 0)
        coupling = matmul(reflect_rows, image_rows, 0, 0)
        shift_term = matmul(middle, coupling, 1, 0)
        companion_rows = image_rows - 0.5 * matmul(reflect_rows, shift_term, 1, 0)
        companion_cols = jnp.take(companion_rows, row_place, axis=0)
        matrix = matrix - matmul(jnp.concatenate((reflect_rows, companion_rows), 1), jnp.concatenate((companion_cols, reflect_cols), 1), 1, 1)
    return matrix
```

```python
import functools
import jax
import jax.numpy as jnp
from jax import lax
from jax.experimental import pallas as pl
from jax.experimental.pallas import tpu as pltpu
from jax.sharding import PartitionSpec as P

B = 256
PANELS = 2
NS_STEPS = 12
INV_STEPS = 5
LEAF = 32
BOTH = ("row", "col")


HIGHEST = lax.Precision.HIGHEST
HIGH = lax.Precision.HIGH


def matmul(first_op, second_op, first_dim, second_dim, precision=HIGH):
    return lax.dot_general(
        first_op,
        second_op,
        (((first_dim,), (second_dim,)), ((), ())),
        precision=precision,
        preferred_element_type=jnp.float32,
    )


def split(value):
    high = value.astype(jnp.bfloat16)
    return high, (value - high.astype(jnp.float32)).astype(jnp.bfloat16)


def dot_split(first_op, second_op, first_dim, second_dim):
    (first_high, first_low), (second_high, second_low) = first_op, second_op
    return lax.dot_general(
        jnp.concatenate((first_high, first_high, first_low), first_dim),
        jnp.concatenate((second_high, second_low, second_high), second_dim),
        (((first_dim,), (second_dim,)), ((), ())),
        preferred_element_type=jnp.float32,
    )


def factor_kernel(gram_ref, top_ref, coef_ref, add_ref, block_ref, work):
    size = gram_ref.shape[0]
    lanes = 128
    row_id = lax.broadcasted_iota(jnp.int32, (size, size), 0)
    col_id = lax.broadcasted_iota(jnp.int32, (size, size), 1)
    eye = (row_id == col_id).astype(jnp.float32)
    work[:, :size] = gram_ref[...]
    work[:, size:] = eye
    leaf_row = lax.broadcasted_iota(jnp.int32, (LEAF, lanes), 0)
    leaf_lane = lax.broadcasted_iota(jnp.int32, (LEAF, lanes), 1)
    for start in range(0, size, LEAF):
        tile = start // lanes * lanes
        offset = start - tile
        part = work[start : start + LEAF, tile : tile + lanes]
        trace = (leaf_row == leaf_lane).astype(jnp.float32)
        for pivot in range(LEAF):
            lane = offset + pivot
            scale = 1.0 / part[pivot : pivot + 1, lane : lane + 1]
            column = jnp.where(leaf_row > pivot, part[:, lane : lane + 1], 0.0)
            part, trace = (
                part - column * (part[pivot : pivot + 1, :] * scale),
                trace - column * (trace[pivot : pivot + 1, :] * scale),
            )
        pivots = jnp.sum(jnp.where(leaf_lane == leaf_row + offset, part, 0.0), axis=1, keepdims=True)
        root = lax.rsqrt(pivots)
        root = root * (1.5 - 0.5 * pivots * root * root)
        leaf_inv = (trace * root)[:, :LEAF]
        low, high = tile, size + tile + lanes
        rows = matmul(leaf_inv, work[start : start + LEAF, low:high], 1, 0, HIGHEST)
        work[start : start + LEAF, low:high] = rows
        below = start + LEAF
        if below < size:
            below_tile = below // lanes * lanes
            change = matmul(rows[:, below_tile - low : size - low], rows, 0, 0, HIGHEST)
            work[below:, low:high] = work[below:, low:high] - change[below - below_tile :, :]
    inverse_low = work[:, size:]
    inverse_up = inverse_low.T
    top_basis = matmul(top_ref[...], inverse_up, 1, 0, HIGHEST)

    def polar_step(step, polar):
        parts = split(polar)
        square = dot_split(parts, parts, 0, 0)
        return 1.5 * polar - 0.5 * dot_split(parts, split(square), 1, 0)

    polar = lax.fori_loop(0, NS_STEPS, polar_step, top_basis)
    polar_parts = split(polar)
    cross = dot_split(polar_parts, split(top_basis), 0, 0)
    metric = eye + cross + cross.T + dot_split(polar_parts, polar_parts, 0, 0)
    metric_parts = split(metric)

    def inverse_step(step, guess):
        parts = split(guess)
        return 2.0 * guess - dot_split(parts, split(dot_split(metric_parts, parts, 1, 0)), 1, 0)

    guess = (40.0 / 41.0) * eye - (8.0 / 41.0) * metric
    middle = split(2.0 * lax.fori_loop(0, INV_STEPS, inverse_step, guess))
    coef_ref[:, :size] = inverse_up
    coef_ref[:, size:] = dot_split(split(inverse_up), middle, 1, 0)
    add_ref[:, :size] = polar
    add_ref[:, size:] = dot_split(polar_parts, middle, 1, 0)
    block_ref[...] = dot_split(split(top_basis + polar), middle, 1, 0)


def factors(gram, top):
    size = gram.shape[0]
    wide = jax.ShapeDtypeStruct((size, 2 * size), jnp.float32)
    return pl.pallas_call(
        factor_kernel,
        out_shape=(wide, wide, jax.ShapeDtypeStruct(gram.shape, jnp.float32)),
        scratch_shapes=[pltpu.VMEM((size, 2 * size), jnp.float32)],
        cost_estimate=pl.CostEstimate(flops=40_000_000_000, bytes_accessed=2_000_000, transcendentals=0),
        name="factors",
    )(gram, top)


def product_of(first_op, second_op, first_dim, second_dim):
    return dot_split(split(first_op), split(second_op), first_dim, second_dim)


def turn_kernel(stride, above, place, block_ref, out_ref):
    tile = block_ref[...].T
    index = pl.program_id(0) * tile.shape[0] + lax.broadcasted_iota(jnp.int32, tile.shape, 0)
    keep = (place[0] == 1) & (index // tile.shape[1] * stride + place[1] > above)
    out_ref[...] = jnp.where(keep, tile, 0.0)


def turn(matrix, row_block, keep, stride, rank, above):
    cols = matrix.shape[1]
    width = min(1024, cols)
    return pl.pallas_call(
        functools.partial(turn_kernel, stride, above),
        out_shape=jax.ShapeDtypeStruct((cols, B), jnp.float32),
        grid_spec=pltpu.PrefetchScalarGridSpec(
            num_scalar_prefetch=1,
            grid=(cols // width,),
            in_specs=[pl.BlockSpec((B, width), lambda i, place: (row_block, i))],
            out_specs=pl.BlockSpec((width, B), lambda i, place: (i, 0)),
        ),
        cost_estimate=pl.CostEstimate(flops=0, bytes_accessed=8 * cols * B, transcendentals=0),
        name="turn",
    )(jnp.stack((keep.astype(jnp.int32), rank.astype(jnp.int32))), matrix)


def reflect_kernel(place, panel_ref, coef_ref, add_ref, *refs):
    reflect_ref, scaled_ref = refs[-3:-1] if len(refs) > 2 else refs
    size = panel_ref.shape[1]
    step = pl.program_id(0)
    both = product_of(panel_ref[...], coef_ref[...], 1, 0)
    reflect_ref[...] = both[:, :size]
    scaled_ref[...] = both[:, size:]
    per = panel_ref.shape[0] // size
    inside = place[0] - step * per

    @pl.when((inside >= 0) & (inside < per))
    def _():
        rows = pl.ds(pl.multiple_of(jnp.clip(inside, 0, per - 1) * size, size), size)
        reflect_ref[rows, :] += add_ref[:, :size]
        scaled_ref[rows, :] += add_ref[:, size:]

    if len(refs) > 2:
        y_ref, q_ref, inner_ref = refs[0], refs[1], refs[-1]

        @pl.when(step == 0)
        def _():
            inner_ref[...] = jnp.zeros_like(inner_ref)

        parts = split(reflect_ref[...])
        inner_ref[:size, :] += dot_split(split(y_ref[...]), parts, 0, 0)
        inner_ref[size:, :] += dot_split(split(q_ref[...]), parts, 0, 0)


def reflect(panel, coef, add, place, before=()):
    size = coef.shape[0]
    rows = min(4 * size, panel.shape[0])
    block = pl.BlockSpec((rows, size), lambda i, place: (i, 0))
    fixed = pl.BlockSpec((size, 2 * size), lambda i, place: (0, 0))
    out = jax.ShapeDtypeStruct(panel.shape, jnp.float32)
    extra = [pl.BlockSpec((2 * size, size), lambda i, place: (0, 0))] if before else []
    return pl.pallas_call(
        reflect_kernel,
        out_shape=[out, out] + [jax.ShapeDtypeStruct((2 * size, size), jnp.float32) for _ in extra],
        grid_spec=pltpu.PrefetchScalarGridSpec(
            num_scalar_prefetch=1,
            grid=(panel.shape[0] // rows,),
            in_specs=[block, fixed, fixed] + [block for _ in before],
            out_specs=[block, block] + extra,
        ),
        cost_estimate=pl.CostEstimate(
            flops=12 * panel.size * size, bytes_accessed=12 * panel.size, transcendentals=0
        ),
        name="reflect",
    )(place.reshape(1), panel, coef, add, *before)


def multiply_kernel(matrix_ref, panel_ref, *refs):
    out_ref, stored = refs[-2:]
    cols = panel_ref.shape[0]
    depth = min(1024, cols)

    @pl.when(pl.program_id(0) == 0)
    def _():
        for start in range(0, cols, depth):
            high, low = split(panel_ref[start : start + depth, :])
            stored[3 * start : 3 * (start + depth), :] = jnp.concatenate((high, low, high), 0)

    total = None
    for start in range(0, cols, depth):
        high, low = split(matrix_ref[:, start : start + depth])
        part = jnp.dot(
            jnp.concatenate((high, high, low), 1),
            stored[3 * start : 3 * (start + depth), :],
            preferred_element_type=jnp.float32,
        )
        total = part if total is None else total + part
    if len(refs) > 2:
        q_ref, y_ref, inner_ref = refs[:3]
        both = jnp.concatenate((q_ref[...], y_ref[...]), 1)
        total = total - product_of(both, inner_ref[...], 1, 0)
    out_ref[...] = total


def multiply(matrix, panel, change=()):
    rows, cols = matrix.shape
    size = panel.shape[1]
    height = min(512, rows)
    side = pl.BlockSpec((height, size), lambda i: (i, 0))
    return pl.pallas_call(
        multiply_kernel,
        out_shape=jax.ShapeDtypeStruct((rows, size), jnp.float32),
        grid=(rows // height,),
        in_specs=[
            pl.BlockSpec((height, cols), lambda i: (i, 0)),
            pl.BlockSpec((cols, size), lambda i: (0, 0), pipeline_mode=pl.Buffered(1)),
        ]
        + ([side, side, pl.BlockSpec((2 * size, size), lambda i: (0, 0))] if change else []),
        out_specs=side,
        scratch_shapes=[pltpu.VMEM((3 * cols, size), jnp.bfloat16)],
        compiler_params=pltpu.CompilerParams(vmem_limit_bytes=60 << 20),
        cost_estimate=pl.CostEstimate(
            flops=6 * rows * cols * size, bytes_accessed=4 * matrix.size, transcendentals=0
        ),
        name="multiply",
    )(matrix, panel, *change)


def interleave(ref, size):
    parts, rows, _ = ref.shape
    if parts == 1:
        return ref[0]
    return jnp.concatenate(
        [
            ref[part, index * size : (index + 1) * size, :]
            for index in range(rows // size)
            for part in range(parts)
        ],
        0,
    )


def companion_kernel(product_ref, scaled_ref, inner_ref, out_ref):
    product = interleave(product_ref, inner_ref.shape[0])
    out_ref[...] = product - product_of(scaled_ref[...], inner_ref[...], 1, 0)


def next_kernel(
    stride, above, grams, rank, product_ref, scaled_ref, inner_ref, raw_ref, left_ref, right_ref, out_ref, next_ref, *gram
):
    size = inner_ref.shape[0]
    step = pl.program_id(0)
    scaled = split(scaled_ref[...])
    companion = interleave(product_ref, size) - dot_split(scaled, split(inner_ref[...]), 1, 0)
    out_ref[...] = companion
    change = dot_split(scaled, split(left_ref[...]), 1, 1) + product_of(companion, right_ref[...], 1, 1)
    index = step * companion.shape[0] + lax.broadcasted_iota(jnp.int32, companion.shape, 0)
    panel = jnp.where(index // size * stride + rank[0] > above, raw_ref[...] - change, 0.0)
    next_ref[...] = panel
    if grams:
        square = matmul(panel, panel, 0, 0, HIGHEST)

        @pl.when(step == 0)
        def _():
            gram[0][...] = square

        @pl.when(step > 0)
        def _():
            gram[0][...] += square


def companion(product, scaled, inner, fold, ahead=None):
    size = inner.shape[0]
    total = scaled.shape[0]
    each = total // fold
    rows = min(max(4 // fold, 1) * size, each)
    source = pl.BlockSpec((fold, rows, size), lambda i, *_: (0, i, 0))
    block = pl.BlockSpec((fold * rows, size), lambda i, *_: (i, 0))
    fixed = pl.BlockSpec((size, size), lambda i, *_: (0, 0))
    out = jax.ShapeDtypeStruct(scaled.shape, jnp.float32)
    product = product.reshape(fold, each, size)
    if ahead is None:
        return pl.pallas_call(
            companion_kernel,
            out_shape=out,
            grid=(each // rows,),
            in_specs=[source, block, fixed],
            out_specs=block,
            cost_estimate=pl.CostEstimate(
                flops=6 * scaled.size * size, bytes_accessed=12 * scaled.size, transcendentals=0
            ),
            name="companion",
        )(product, scaled, inner)
    raw, y_block, q_block, stride, above, rank, grams = ahead
    return pl.pallas_call(
        functools.partial(next_kernel, stride, above, grams),
        out_shape=(out, out) + ((jax.ShapeDtypeStruct((size, size), jnp.float32),) if grams else ()),
        grid_spec=pltpu.PrefetchScalarGridSpec(
            num_scalar_prefetch=1,
            grid=(each // rows,),
            in_specs=[source, block, fixed, block, fixed, fixed],
            out_specs=[block, block] + ([fixed] if grams else []),
        ),
        cost_estimate=pl.CostEstimate(
            flops=30 * scaled.size * size, bytes_accessed=20 * scaled.size, transcendentals=0
        ),
        name="companion_next",
    )(rank.reshape(1), product, scaled, inner, raw, y_block, q_block)


def update_kernel(matrix_ref, q_rows_ref, y_rows_ref, q_cols_ref, y_cols_ref, out_ref, left, right):
    col_step, row_step = pl.program_id(0), pl.program_id(1)
    height, width = matrix_ref.shape
    rows = pl.ds(pl.multiple_of(row_step * height, height), height)

    @pl.when(row_step == 0)
    def _():
        high, low = split(jnp.concatenate((y_cols_ref[...], q_cols_ref[...]), 1).T)
        right[...] = jnp.concatenate((high, low, high), 0)

    @pl.when(col_step == 0)
    def _():
        high, low = split(jnp.concatenate((q_rows_ref[...], y_rows_ref[...]), 1))
        left[rows, :] = jnp.concatenate((high, high, low), 1)

    span = q_rows_ref.shape[1]
    for start in range(0, width, span):
        change = jnp.dot(left[rows, :], right[:, start : start + span], preferred_element_type=jnp.float32)
        out_ref[:, start : start + span] = matrix_ref[:, start : start + span] - change


def update(matrix, q_rows, y_rows, q_cols, y_cols):
    size = q_rows.shape[1]
    rows, cols = matrix.shape
    height, width = min(1024, rows), min(1024, cols)
    tile = pl.BlockSpec((height, width), lambda j, i: (i, j))
    row_side = pl.BlockSpec((height, size), lambda j, i: (i, 0))
    col_side = pl.BlockSpec((width, size), lambda j, i: (j, 0))
    return pl.pallas_call(
        update_kernel,
        out_shape=jax.ShapeDtypeStruct(matrix.shape, jnp.float32),
        grid=(cols // width, rows // height),
        in_specs=[tile, row_side, row_side, col_side, col_side],
        out_specs=tile,
        scratch_shapes=[
            pltpu.VMEM((rows, 6 * size), jnp.bfloat16),
            pltpu.VMEM((6 * size, width), jnp.bfloat16),
        ],
        compiler_params=pltpu.CompilerParams(vmem_limit_bytes=60 << 20),
        cost_estimate=pl.CostEstimate(
            flops=12 * rows * cols * size, bytes_accessed=8 * matrix.size, transcendentals=0
        ),
        name="update",
    )(matrix, q_rows, y_rows, q_cols, y_cols)


def tie(*arrays):
    return lax.optimization_barrier(arrays)


def lockstep(*tasks):
    results = [None] * len(tasks)
    states = {}

    def advance(place, *state):
        task = tasks[place]
        try:
            if isinstance(task, tuple) and not state:
                states[place] = task[0].send(task[1])
            elif isinstance(task, tuple):
                states[place] = task[0].send(*state)
            else:
                states[place] = task.send(*state) if state else next(task)
        except StopIteration as stop:
            results[place] = stop.value
            states.pop(place, None)

    for place in range(len(tasks)):
        advance(place)
    while states:
        flat, tree = jax.tree.flatten(states)
        ended = jax.tree.unflatten(tree, tie(*flat)) if flat else dict(states)
        for place in list(ended):
            advance(place, ended[place])
    return results


class Grid:
    def __init__(self):
        self.rows = lax.axis_size("row")
        self.cols = lax.axis_size("col")
        self.p = lax.axis_index("row")
        self.q = lax.axis_index("col")
        self.first = self.p % 2 == 0
        self.row_bits = [1 << bit for bit in range(1, self.rows.bit_length() - 1)]
        self.col_bits = [1 << bit for bit in range(self.cols.bit_length() - 1)]

    def swap(self, array, row_bit=0, col_bit=0, only=None):
        pairs = [
            (p * self.cols + q, (p ^ row_bit) * self.cols + (q ^ col_bit))
            for p in range(self.rows)
            for q in range(self.cols)
            if only is None or only(p, q)
        ]
        return lax.ppermute(array, BOTH, pairs)

    def halves(self, low, high):
        return jnp.where(self.first, low, high), jnp.where(self.first, high, low)

    def sum_core(self, array):
        half = array.shape[0] // 2
        kept, sent = self.halves(array[:half], array[half:])
        return kept + self.swap(sent, 1)

    def join_core(self, kept, other):
        low, high = self.halves(kept, other)
        return jnp.concatenate((low, high), 0)

    def spread_rows(self, array, owner):
        bits = self.col_bits
        parts = jnp.split(array, len(bits), 0)
        spans = [{owner} for _ in parts]
        for stage in range(len(bits)):
            new = []
            for turn, part in enumerate(parts):
                bit = bits[(turn + stage) % len(bits)]
                span = spans[turn]
                got = self.swap(part, 0, bit, lambda p, q: q in span)
                fresh = {q ^ bit for q in span}
                is_fresh = functools.reduce(jnp.logical_or, [self.q == q for q in sorted(fresh)])
                new.append(jnp.where(is_fresh, got, part))
                spans[turn] = span | fresh
            parts = yield new
        return jnp.concatenate(parts, 0)

    def sum_scatter(self, array):
        bits = self.col_bits
        count = len(bits)
        whole = array.reshape(*(2,) * count, count, -1, array.shape[1])
        parts = [whole[(slice(None),) * count + (turn,)] for turn in range(count)]
        left = [list(bits[::-1])] * count
        for stage in range(count):
            new = []
            for turn, part in enumerate(parts):
                bit = bits[(turn + stage) % count]
                axis = left[turn].index(bit)
                left[turn] = [other for other in left[turn] if other != bit]
                is_high = (self.q & bit) != 0
                low, high = (lax.index_in_dim(part, side, axis, False) for side in (0, 1))
                got = self.swap(jnp.where(is_high, low, high), 0, bit)
                new.append(jnp.where(is_high, high, low) + got)
            parts = yield new
        return parts

    def gather_rows(self, parts, width):
        bits = self.col_bits
        count = len(bits)
        orders = [[bits[(turn + stage) % count] for stage in range(count)] for turn in range(count)]
        held = [[] for _ in parts]
        for stage in reversed(range(count)):
            new = []
            for turn, part in enumerate(parts):
                bit = orders[turn][stage]
                held[turn] = sorted(held[turn] + [bit], reverse=True)
                axis = held[turn].index(bit)
                got = self.swap(part, 0, bit)
                is_high = (self.q & bit) != 0
                low, high = jnp.where(is_high, got, part), jnp.where(is_high, part, got)
                new.append(jnp.stack((low, high), axis))
            parts = yield new
        return jnp.stack(parts, count).reshape(-1, width)

    def gather_cols(self, piece):
        pairs = [
            (p * self.cols + q, (p // self.cols * self.cols + q) * self.cols + p % self.cols)
            for p in range(self.rows)
            for q in range(self.cols)
        ]
        (moved,) = yield [lax.ppermute(piece, BOTH, pairs)]
        return lax.all_gather(moved, "row", tiled=True)


def block_of(index, count):
    return index % count, index // count * B


def body(affinity):
    grid = Grid()
    rows_here, cols_here = affinity.shape
    row_blocks = jnp.arange(rows_here, dtype=jnp.int32) // B * grid.rows + grid.p
    col_blocks = jnp.arange(cols_here, dtype=jnp.int32) // B * grid.cols + grid.q
    matrix = affinity

    def column_of(panel):
        owner, start = block_of(panel, grid.cols)
        return matrix[:, start : start + B], owner

    def row_of(panel, above):
        owner, start = block_of(panel, grid.rows)
        return turn(matrix, start // B, grid.p == owner, grid.cols, grid.q, above)

    top_p, top_row = block_of(1, grid.rows)
    owned, owner = column_of(0)
    owned = jnp.where((row_blocks > 0)[:, None], owned, 0.0)
    mine = (grid.q == owner).astype(jnp.float32)
    square = mine * matmul(owned, owned, 0, 0, HIGHEST)
    top = mine * (grid.p == top_p) * owned[top_row : top_row + B]
    sums, block = tie(jnp.concatenate((square, top), 1), row_of(0, 0))
    panel_cols = lax.psum(block, "row")
    sums = grid.sum_core(sums)
    for bit in grid.row_bits:
        sums = sums + grid.swap(sums, bit)
    rows_task = grid.spread_rows(owned, owner)
    sums, *state = tie(sums, *next(rows_task))
    for bit in grid.col_bits:
        sums = sums + grid.swap(sums, 0, bit)
    sums = grid.join_core(sums, grid.swap(sums, 1))
    sums, *state = tie(sums, *state)
    (panel_rows,) = lockstep((rows_task, state))

    fold = grid.rows // grid.cols
    before = None
    for panel in range(PANELS):
        last = panel + 1 == PANELS
        top_p, top_row = block_of(panel + 1, grid.rows)
        top_q, top_col = block_of(panel + 1, grid.cols)
        coef, add, q_block = factors(sums[:, :B], sums[:, B:])
        place_row = jnp.where(grid.p == top_p, top_row // B, -1)
        place_col = jnp.where(grid.q == top_q, top_col // B, -1)
        if not last:
            ahead_block, ahead_column, panel_cols, coef = tie(
                row_of(panel + 1, -1), column_of(panel + 1)[0], panel_cols, coef
            )
            raw_cols = lax.psum(ahead_block, "row")
            rows_task = grid.spread_rows(ahead_column, block_of(panel + 1, grid.cols)[0])
            state = next(rows_task)
        if before is None:
            reflect_cols, q_cols = reflect(panel_cols, coef, add, place_col)
            local = multiply(matrix, reflect_cols)
        else:
            last_q_rows, last_y_rows, last_q_cols, last_y_cols = before
            reflect_cols, q_cols, cross = reflect(
                panel_cols, coef, add, place_col, (last_y_cols, last_q_cols)
            )
            local = multiply(matrix, reflect_cols, (last_q_rows, last_y_rows, cross))
        reflect_rows, q_rows = reflect(panel_rows, coef, add, place_row)
        inner = matmul(reflect_rows, local, 0, 0)
        if last:
            tasks = [product_task(grid, local), inner_task(grid, inner)]
        else:
            local, *state = tie(local, *state)
            tasks = [
                product_task(grid, local),
                inner_task(grid, inner, raw_cols, reflect_cols),
                ahead_rows_task(grid, rows_task, state),
            ]
        if before is not None:
            tasks.append(update_task(grid, matrix, before))
        results = lockstep(*tasks)
        product_rows, product_cols = results[0]
        inner = results[1]
        half_inner = 0.5 * inner[:, :B]
        if before is not None:
            matrix, product_cols = tie(results[-1], product_cols)
        if last:
            y_rows = companion(product_rows, q_rows, half_inner, 1)
            y_cols = companion(product_cols, q_cols, half_inner, fold)
        else:
            y_block = inner[:, B:] - matmul(q_block, half_inner, 1, 0)
            y_cols, panel_cols, square = companion(
                product_cols, q_cols, half_inner, fold,
                (raw_cols, y_block, q_block, grid.cols, panel + 1, grid.q, True),
            )
            next_q, next_col = block_of(panel + 2, grid.cols)
            top = (grid.q == next_q) * panel_cols[next_col : next_col + B]
            sums = jnp.concatenate((square, top), 1)
            half = B // 2
            sums = grid.halves(sums[:half], sums[half:])[0]
            for bit in grid.col_bits:
                sums = sums + grid.swap(sums, 0, bit)
            sums = grid.join_core(sums, grid.swap(sums, 1))
            y_rows, panel_rows = companion(
                product_rows, q_rows, half_inner, 1,
                (results[2], y_block, q_block, grid.rows, panel + 1, grid.p, False),
            )
        before = (q_rows, y_rows, q_cols, y_cols)
    return update(matrix, *before)


def product_task(grid, local):
    parts = yield from grid.sum_scatter(local)
    piece = jnp.stack(parts).reshape(-1, local.shape[1])
    cols_task = grid.gather_cols(piece)
    (moved,) = yield next(cols_task)
    try:
        cols_task.send([moved])
    except StopIteration as stop:
        product_cols = stop.value
    product_rows = yield from grid.gather_rows(parts, local.shape[1])
    return product_rows, product_cols


def idle(stages):
    for _ in range(stages):
        yield []


def inner_task(grid, inner, raw_cols=None, reflect_cols=None):
    (inner,) = yield [grid.sum_core(inner)]
    for bit in grid.row_bits:
        (inner,) = yield [inner + grid.swap(inner, bit)]
    if raw_cols is not None:
        block = matmul(raw_cols, reflect_cols, 0, 0)
        half = B // 2
        inner = jnp.concatenate((inner, grid.halves(block[:half], block[half:])[0]), 1)
    for bit in grid.col_bits:
        (inner,) = yield [inner + grid.swap(inner, 0, bit)]
    (other,) = yield [grid.swap(inner, 1)]
    return grid.join_core(inner, other)


def ahead_rows_task(grid, task, state):
    yield from idle(len(grid.col_bits) + 1)
    while True:
        try:
            state = task.send(state)
        except StopIteration as stop:
            return stop.value
        state = yield state


def update_task(grid, matrix, before):
    yield from idle(len(grid.col_bits))
    (first,) = yield [before[0]]
    return update(matrix, first, *before[1:])


def solution(mesh):
    return jax.shard_map(
        body,
        mesh=mesh,
        in_specs=(P("row", "col"),),
        out_specs=P("row", "col"),
        check_vma=False,
    )
```

```python
import functools
import jax
import jax.numpy as jnp
from jax import lax
from jax.experimental import pallas as pl
from jax.experimental.pallas import tpu as pltpu
from jax.sharding import PartitionSpec as P

B = 256
PANELS = 2
NS_STEPS = 12
INV_STEPS = 5
LEAF = 64
BOTH = ("row", "col")


HIGHEST = lax.Precision.HIGHEST
HIGH = lax.Precision.HIGH


def matmul(first_op, second_op, first_dim, second_dim, precision=HIGH):
    return lax.dot_general(
        first_op,
        second_op,
        (((first_dim,), (second_dim,)), ((), ())),
        precision=precision,
        preferred_element_type=jnp.float32,
    )


def split(value):
    high = value.astype(jnp.bfloat16)
    return high, (value - high.astype(jnp.float32)).astype(jnp.bfloat16)


def dot_split(first_op, second_op, first_dim, second_dim):
    (first_high, first_low), (second_high, second_low) = first_op, second_op
    return lax.dot_general(
        jnp.concatenate((first_high, first_high, first_low), first_dim),
        jnp.concatenate((second_high, second_low, second_high), second_dim),
        (((first_dim,), (second_dim,)), ((), ())),
        preferred_element_type=jnp.float32,
    )


def factor_kernel(gram_ref, top_ref, coef_ref, add_ref, block_ref, work):
    size = gram_ref.shape[0]
    lanes = 128
    row_id = lax.broadcasted_iota(jnp.int32, (size, size), 0)
    col_id = lax.broadcasted_iota(jnp.int32, (size, size), 1)
    eye = (row_id == col_id).astype(jnp.float32)
    work[:, :size] = gram_ref[...]
    work[:, size:] = eye
    leaf_row = lax.broadcasted_iota(jnp.int32, (LEAF, lanes), 0)
    leaf_lane = lax.broadcasted_iota(jnp.int32, (LEAF, lanes), 1)
    for start in range(0, size, LEAF):
        tile = start // lanes * lanes
        offset = start - tile
        part = work[start : start + LEAF, tile : tile + lanes]
        trace = (leaf_row == leaf_lane).astype(jnp.float32)
        for pivot in range(LEAF):
            lane = offset + pivot
            scale = 1.0 / part[pivot : pivot + 1, lane : lane + 1]
            column = jnp.where(leaf_row > pivot, part[:, lane : lane + 1], 0.0)
            part, trace = (
                part - column * (part[pivot : pivot + 1, :] * scale),
                trace - column * (trace[pivot : pivot + 1, :] * scale),
            )
        pivots = jnp.sum(jnp.where(leaf_lane == leaf_row + offset, part, 0.0), axis=1, keepdims=True)
        root = lax.rsqrt(pivots)
        root = root * (1.5 - 0.5 * pivots * root * root)
        leaf_inv = (trace * root)[:, :LEAF]
        low, high = tile, size + tile + lanes
        rows = matmul(leaf_inv, work[start : start + LEAF, low:high], 1, 0, HIGHEST)
        work[start : start + LEAF, low:high] = rows
        below = start + LEAF
        if below < size:
            below_tile = below // lanes * lanes
            change = matmul(rows[:, below_tile - low : size - low], rows, 0, 0, HIGHEST)
            work[below:, low:high] = work[below:, low:high] - change[below - below_tile :, :]
    inverse_low = work[:, size:]
    inverse_up = inverse_low.T
    top_basis = matmul(top_ref[...], inverse_up, 1, 0, HIGHEST)

    def polar_step(step, polar):
        parts = split(polar)
        square = dot_split(parts, parts, 0, 0)
        return 1.5 * polar - 0.5 * dot_split(parts, split(square), 1, 0)

    polar = lax.fori_loop(0, NS_STEPS, polar_step, top_basis)
    polar_parts = split(polar)
    cross = dot_split(polar_parts, split(top_basis), 0, 0)
    metric = eye + cross + cross.T + dot_split(polar_parts, polar_parts, 0, 0)
    metric_parts = split(metric)

    def inverse_step(step, guess):
        parts = split(guess)
        return 2.0 * guess - dot_split(parts, split(dot_split(metric_parts, parts, 1, 0)), 1, 0)

    guess = (40.0 / 41.0) * eye - (8.0 / 41.0) * metric
    middle = split(2.0 * lax.fori_loop(0, INV_STEPS, inverse_step, guess))
    coef_ref[:, :size] = inverse_up
    coef_ref[:, size:] = dot_split(split(inverse_up), middle, 1, 0)
    add_ref[:, :size] = polar
    add_ref[:, size:] = dot_split(polar_parts, middle, 1, 0)
    block_ref[...] = dot_split(split(top_basis + polar), middle, 1, 0)


def factors(gram, top):
    size = gram.shape[0]
    wide = jax.ShapeDtypeStruct((size, 2 * size), jnp.float32)
    return pl.pallas_call(
        factor_kernel,
        out_shape=(wide, wide, jax.ShapeDtypeStruct(gram.shape, jnp.float32)),
        scratch_shapes=[pltpu.VMEM((size, 2 * size), jnp.float32)],
        cost_estimate=pl.CostEstimate(flops=40_000_000_000, bytes_accessed=2_000_000, transcendentals=0),
        name="factors",
    )(gram, top)


def product_of(first_op, second_op, first_dim, second_dim):
    return dot_split(split(first_op), split(second_op), first_dim, second_dim)


def turn_kernel(stride, above, place, block_ref, out_ref):
    tile = block_ref[...].T
    index = pl.program_id(0) * tile.shape[0] + lax.broadcasted_iota(jnp.int32, tile.shape, 0)
    keep = (place[0] == 1) & (index // tile.shape[1] * stride + place[1] > above)
    out_ref[...] = jnp.where(keep, tile, 0.0)


def turn(matrix, row_block, keep, stride, rank, above):
    cols = matrix.shape[1]
    width = min(1024, cols)
    return pl.pallas_call(
        functools.partial(turn_kernel, stride, above),
        out_shape=jax.ShapeDtypeStruct((cols, B), jnp.float32),
        grid_spec=pltpu.PrefetchScalarGridSpec(
            num_scalar_prefetch=1,
            grid=(cols // width,),
            in_specs=[pl.BlockSpec((B, width), lambda i, place: (row_block, i))],
            out_specs=pl.BlockSpec((width, B), lambda i, place: (i, 0)),
        ),
        cost_estimate=pl.CostEstimate(flops=0, bytes_accessed=8 * cols * B, transcendentals=0),
        name="turn",
    )(jnp.stack((keep.astype(jnp.int32), rank.astype(jnp.int32))), matrix)


def reflect_kernel(place, panel_ref, coef_ref, add_ref, *refs):
    reflect_ref, scaled_ref = refs[-3:-1] if len(refs) > 2 else refs
    size = panel_ref.shape[1]
    step = pl.program_id(0)
    both = product_of(panel_ref[...], coef_ref[...], 1, 0)
    reflect_ref[...] = both[:, :size]
    scaled_ref[...] = both[:, size:]
    per = panel_ref.shape[0] // size
    inside = place[0] - step * per

    @pl.when((inside >= 0) & (inside < per))
    def _():
        rows = pl.ds(pl.multiple_of(jnp.clip(inside, 0, per - 1) * size, size), size)
        reflect_ref[rows, :] += add_ref[:, :size]
        scaled_ref[rows, :] += add_ref[:, size:]

    if len(refs) > 2:
        y_ref, q_ref, inner_ref = refs[0], refs[1], refs[-1]

        @pl.when(step == 0)
        def _():
            inner_ref[...] = jnp.zeros_like(inner_ref)

        parts = split(reflect_ref[...])
        inner_ref[:size, :] += dot_split(split(y_ref[...]), parts, 0, 0)
        inner_ref[size:, :] += dot_split(split(q_ref[...]), parts, 0, 0)


def reflect(panel, coef, add, place, before=()):
    size = coef.shape[0]
    rows = min(4 * size, panel.shape[0])
    block = pl.BlockSpec((rows, size), lambda i, place: (i, 0))
    fixed = pl.BlockSpec((size, 2 * size), lambda i, place: (0, 0))
    out = jax.ShapeDtypeStruct(panel.shape, jnp.float32)
    extra = [pl.BlockSpec((2 * size, size), lambda i, place: (0, 0))] if before else []
    return pl.pallas_call(
        reflect_kernel,
        out_shape=[out, out] + [jax.ShapeDtypeStruct((2 * size, size), jnp.float32) for _ in extra],
        grid_spec=pltpu.PrefetchScalarGridSpec(
            num_scalar_prefetch=1,
            grid=(panel.shape[0] // rows,),
            in_specs=[block, fixed, fixed] + [block for _ in before],
            out_specs=[block, block] + extra,
        ),
        cost_estimate=pl.CostEstimate(
            flops=12 * panel.size * size, bytes_accessed=12 * panel.size, transcendentals=0
        ),
        name="reflect",
    )(place.reshape(1), panel, coef, add, *before)


def multiply_kernel(matrix_ref, panel_ref, *refs):
    out_ref, stored = refs[-2:]
    cols = panel_ref.shape[0]
    depth = min(1024, cols)

    @pl.when(pl.program_id(0) == 0)
    def _():
        for start in range(0, cols, depth):
            high, low = split(panel_ref[start : start + depth, :])
            stored[3 * start : 3 * (start + depth), :] = jnp.concatenate((high, low, high), 0)

    total = None
    for start in range(0, cols, depth):
        high, low = split(matrix_ref[:, start : start + depth])
        part = jnp.dot(
            jnp.concatenate((high, high, low), 1),
            stored[3 * start : 3 * (start + depth), :],
            preferred_element_type=jnp.float32,
        )
        total = part if total is None else total + part
    if len(refs) > 2:
        q_ref, y_ref, inner_ref = refs[:3]
        both = jnp.concatenate((q_ref[...], y_ref[...]), 1)
        total = total - product_of(both, inner_ref[...], 1, 0)
    out_ref[...] = total


def multiply(matrix, panel, change=()):
    rows, cols = matrix.shape
    size = panel.shape[1]
    height = min(512, rows)
    side = pl.BlockSpec((height, size), lambda i: (i, 0))
    return pl.pallas_call(
        multiply_kernel,
        out_shape=jax.ShapeDtypeStruct((rows, size), jnp.float32),
        grid=(rows // height,),
        in_specs=[
            pl.BlockSpec((height, cols), lambda i: (i, 0)),
            pl.BlockSpec((cols, size), lambda i: (0, 0), pipeline_mode=pl.Buffered(1)),
        ]
        + ([side, side, pl.BlockSpec((2 * size, size), lambda i: (0, 0))] if change else []),
        out_specs=side,
        scratch_shapes=[pltpu.VMEM((3 * cols, size), jnp.bfloat16)],
        compiler_params=pltpu.CompilerParams(vmem_limit_bytes=60 << 20),
        cost_estimate=pl.CostEstimate(
            flops=6 * rows * cols * size, bytes_accessed=4 * matrix.size, transcendentals=0
        ),
        name="multiply",
    )(matrix, panel, *change)


def interleave(ref, size):
    parts, rows, _ = ref.shape
    if parts == 1:
        return ref[0]
    return jnp.concatenate(
        [
            ref[part, index * size : (index + 1) * size, :]
            for index in range(rows // size)
            for part in range(parts)
        ],
        0,
    )


def companion_kernel(product_ref, scaled_ref, inner_ref, out_ref):
    product = interleave(product_ref, inner_ref.shape[0])
    out_ref[...] = product - product_of(scaled_ref[...], inner_ref[...], 1, 0)


def next_kernel(
    stride, above, grams, rank, product_ref, scaled_ref, inner_ref, raw_ref, left_ref, right_ref, out_ref, next_ref, *gram
):
    size = inner_ref.shape[0]
    step = pl.program_id(0)
    scaled = split(scaled_ref[...])
    companion = interleave(product_ref, size) - dot_split(scaled, split(inner_ref[...]), 1, 0)
    out_ref[...] = companion
    change = dot_split(scaled, split(left_ref[...]), 1, 1) + product_of(companion, right_ref[...], 1, 1)
    index = step * companion.shape[0] + lax.broadcasted_iota(jnp.int32, companion.shape, 0)
    panel = jnp.where(index // size * stride + rank[0] > above, raw_ref[...] - change, 0.0)
    next_ref[...] = panel
    if grams:
        square = matmul(panel, panel, 0, 0, HIGHEST)

        @pl.when(step == 0)
        def _():
            gram[0][...] = square

        @pl.when(step > 0)
        def _():
            gram[0][...] += square


def companion(product, scaled, inner, fold, ahead=None):
    size = inner.shape[0]
    total = scaled.shape[0]
    each = total // fold
    rows = min(max(4 // fold, 1) * size, each)
    source = pl.BlockSpec((fold, rows, size), lambda i, *_: (0, i, 0))
    block = pl.BlockSpec((fold * rows, size), lambda i, *_: (i, 0))
    fixed = pl.BlockSpec((size, size), lambda i, *_: (0, 0))
    out = jax.ShapeDtypeStruct(scaled.shape, jnp.float32)
    product = product.reshape(fold, each, size)
    if ahead is None:
        return pl.pallas_call(
            companion_kernel,
            out_shape=out,
            grid=(each // rows,),
            in_specs=[source, block, fixed],
            out_specs=block,
            cost_estimate=pl.CostEstimate(
                flops=6 * scaled.size * size, bytes_accessed=12 * scaled.size, transcendentals=0
            ),
            name="companion",
        )(product, scaled, inner)
    raw, y_block, q_block, stride, above, rank, grams = ahead
    return pl.pallas_call(
        functools.partial(next_kernel, stride, above, grams),
        out_shape=(out, out) + ((jax.ShapeDtypeStruct((size, size), jnp.float32),) if grams else ()),
        grid_spec=pltpu.PrefetchScalarGridSpec(
            num_scalar_prefetch=1,
            grid=(each // rows,),
            in_specs=[source, block, fixed, block, fixed, fixed],
            out_specs=[block, block] + ([fixed] if grams else []),
        ),
        cost_estimate=pl.CostEstimate(
            flops=30 * scaled.size * size, bytes_accessed=20 * scaled.size, transcendentals=0
        ),
        name="companion_next",
    )(rank.reshape(1), product, scaled, inner, raw, y_block, q_block)


def update_kernel(matrix_ref, q_rows_ref, y_rows_ref, q_cols_ref, y_cols_ref, *refs):
    out_ref, right = refs[-2:]
    size = q_rows_ref.shape[1]
    cols = matrix_ref.shape[1]
    width = 2 * size

    @pl.when(pl.program_id(0) == 0)
    def _():
        def fill(index, carry):
            span = pl.ds(pl.multiple_of(index * width, width), width)
            high, low = split(jnp.concatenate((y_cols_ref[span, :], q_cols_ref[span, :]), 1).T)
            right[:, span] = jnp.concatenate((high, low, high), 0)
            return carry

        lax.fori_loop(0, cols // width, fill, 0)

    high, low = split(jnp.concatenate((q_rows_ref[...], y_rows_ref[...]), 1))
    left = jnp.concatenate((high, high, low), 1)

    def piece(index, carry):
        span = pl.ds(pl.multiple_of(index * width, width), width)
        change = jnp.dot(left, right[:, span], preferred_element_type=jnp.float32)
        out_ref[:, span] = matrix_ref[:, span] - change
        return carry

    lax.fori_loop(0, cols // width, piece, 0)


def update(matrix, q_rows, y_rows, q_cols, y_cols, span=(0, 1), into=None):
    size = q_rows.shape[1]
    rows, cols = matrix.shape
    part, parts = span
    steps = rows // size // parts
    start = part * steps
    tile = pl.BlockSpec((size, cols), lambda i: (start + i, 0))
    side = pl.BlockSpec((size, size), lambda i: (start + i, 0))
    whole = pl.BlockSpec((cols, size), lambda i: (0, 0), pipeline_mode=pl.Buffered(1))
    extra = [] if into is None else [into]
    return pl.pallas_call(
        update_kernel,
        out_shape=jax.ShapeDtypeStruct(matrix.shape, jnp.float32),
        grid=(steps,),
        in_specs=[tile, side, side, whole, whole] + [pl.BlockSpec(memory_space=pl.ANY) for _ in extra],
        out_specs=tile,
        scratch_shapes=[pltpu.VMEM((6 * size, cols), jnp.bfloat16)],
        input_output_aliases={5: 0} if extra else {},
        compiler_params=pltpu.CompilerParams(vmem_limit_bytes=60 << 20),
        cost_estimate=pl.CostEstimate(
            flops=12 * rows * cols * size // parts,
            bytes_accessed=8 * matrix.size // parts,
            transcendentals=0,
        ),
        name="update",
    )(matrix, q_rows, y_rows, q_cols, y_cols, *extra)


def tie(*arrays):
    return lax.optimization_barrier(arrays)


def lockstep(*tasks):
    results = [None] * len(tasks)
    states = {}

    def advance(place, *state):
        task = tasks[place]
        try:
            if isinstance(task, tuple) and not state:
                states[place] = task[0].send(task[1])
            elif isinstance(task, tuple):
                states[place] = task[0].send(*state)
            else:
                states[place] = task.send(*state) if state else next(task)
        except StopIteration as stop:
            results[place] = stop.value
            states.pop(place, None)

    for place in range(len(tasks)):
        advance(place)
    while states:
        flat, tree = jax.tree.flatten(states)
        ended = jax.tree.unflatten(tree, tie(*flat)) if flat else dict(states)
        for place in list(ended):
            advance(place, ended[place])
    return results


class Grid:
    def __init__(self):
        self.rows = lax.axis_size("row")
        self.cols = lax.axis_size("col")
        self.p = lax.axis_index("row")
        self.q = lax.axis_index("col")
        self.first = self.p % 2 == 0
        self.row_bits = [1 << bit for bit in range(1, self.rows.bit_length() - 1)]
        self.col_bits = [1 << bit for bit in range(self.cols.bit_length() - 1)]

    def swap(self, array, row_bit=0, col_bit=0, only=None):
        pairs = [
            (p * self.cols + q, (p ^ row_bit) * self.cols + (q ^ col_bit))
            for p in range(self.rows)
            for q in range(self.cols)
            if only is None or only(p, q)
        ]
        return lax.ppermute(array, BOTH, pairs)

    def halves(self, low, high):
        return jnp.where(self.first, low, high), jnp.where(self.first, high, low)

    def sum_core(self, array):
        half = array.shape[0] // 2
        kept, sent = self.halves(array[:half], array[half:])
        return kept + self.swap(sent, 1)

    def join_core(self, kept, other):
        low, high = self.halves(kept, other)
        return jnp.concatenate((low, high), 0)

    def spread_rows(self, array, owner):
        bits = self.col_bits
        parts = jnp.split(array, len(bits), 0)
        spans = [{owner} for _ in parts]
        for stage in range(len(bits)):
            new = []
            for turn, part in enumerate(parts):
                bit = bits[(turn + stage) % len(bits)]
                span = spans[turn]
                got = self.swap(part, 0, bit, lambda p, q: q in span)
                fresh = {q ^ bit for q in span}
                is_fresh = functools.reduce(jnp.logical_or, [self.q == q for q in sorted(fresh)])
                new.append(jnp.where(is_fresh, got, part))
                spans[turn] = span | fresh
            parts = yield new
        return jnp.concatenate(parts, 0)

    def sum_scatter(self, array):
        bits = self.col_bits
        count = len(bits)
        whole = array.reshape(*(2,) * count, count, -1, array.shape[1])
        parts = [whole[(slice(None),) * count + (turn,)] for turn in range(count)]
        left = [list(bits[::-1])] * count
        for stage in range(count):
            new = []
            for turn, part in enumerate(parts):
                bit = bits[(turn + stage) % count]
                axis = left[turn].index(bit)
                left[turn] = [other for other in left[turn] if other != bit]
                is_high = (self.q & bit) != 0
                low, high = (lax.index_in_dim(part, side, axis, False) for side in (0, 1))
                got = self.swap(jnp.where(is_high, low, high), 0, bit)
                new.append(jnp.where(is_high, high, low) + got)
            parts = yield new
        return parts

    def gather_rows(self, parts, width):
        bits = self.col_bits
        count = len(bits)
        orders = [[bits[(turn + stage) % count] for stage in range(count)] for turn in range(count)]
        held = [[] for _ in parts]
        for stage in reversed(range(count)):
            new = []
            for turn, part in enumerate(parts):
                bit = orders[turn][stage]
                held[turn] = sorted(held[turn] + [bit], reverse=True)
                axis = held[turn].index(bit)
                got = self.swap(part, 0, bit)
                is_high = (self.q & bit) != 0
                low, high = jnp.where(is_high, got, part), jnp.where(is_high, part, got)
                new.append(jnp.stack((low, high), axis))
            parts = yield new
        return jnp.stack(parts, count).reshape(-1, width)

    def gather_cols(self, piece):
        pairs = [
            (p * self.cols + q, (p // self.cols * self.cols + q) * self.cols + p % self.cols)
            for p in range(self.rows)
            for q in range(self.cols)
        ]
        (moved,) = yield [lax.ppermute(piece, BOTH, pairs)]
        return lax.all_gather(moved, "row", tiled=True)


def block_of(index, count):
    return index % count, index // count * B


def body(affinity):
    grid = Grid()
    rows_here, cols_here = affinity.shape
    row_blocks = jnp.arange(rows_here, dtype=jnp.int32) // B * grid.rows + grid.p
    col_blocks = jnp.arange(cols_here, dtype=jnp.int32) // B * grid.cols + grid.q
    matrix = affinity

    def column_of(panel):
        owner, start = block_of(panel, grid.cols)
        return matrix[:, start : start + B], owner

    def row_of(panel, above):
        owner, start = block_of(panel, grid.rows)
        return turn(matrix, start // B, grid.p == owner, grid.cols, grid.q, above)

    top_p, top_row = block_of(1, grid.rows)
    owned, owner = column_of(0)
    owned, block = tie(owned, row_of(0, 0))
    panel_cols = lax.psum(block, "row")
    owned = jnp.where((row_blocks > 0)[:, None], owned, 0.0)
    mine = (grid.q == owner).astype(jnp.float32)
    square = mine * matmul(owned, owned, 0, 0, HIGHEST)
    top = mine * (grid.p == top_p) * owned[top_row : top_row + B]
    sums = grid.sum_core(jnp.concatenate((square, top), 1))
    ahead_block = row_of(1, -1)
    for bit in grid.row_bits:
        sums = sums + grid.swap(sums, bit)
        sums, ahead_block = tie(sums, ahead_block)
    rows_task = grid.spread_rows(owned, owner)
    sums, *state = tie(sums, *next(rows_task))
    for bit in grid.col_bits:
        sums = sums + grid.swap(sums, 0, bit)
    sums = grid.join_core(sums, grid.swap(sums, 1))
    sums, *state = tie(sums, *state)
    (panel_rows,) = lockstep((rows_task, state))

    fold = grid.rows // grid.cols
    before = None
    for panel in range(PANELS):
        last = panel + 1 == PANELS
        top_p, top_row = block_of(panel + 1, grid.rows)
        top_q, top_col = block_of(panel + 1, grid.cols)
        coef, add, q_block = factors(sums[:, :B], sums[:, B:])
        place_row = jnp.where(grid.p == top_p, top_row // B, -1)
        place_col = jnp.where(grid.q == top_q, top_col // B, -1)
        if not last:
            ahead_column, owner = column_of(panel + 1)
            ahead_block, ahead_column, panel_cols, coef = tie(
                ahead_block, ahead_column, panel_cols, coef
            )
            raw_cols = lax.psum(ahead_block, "row")
            ahead_task = grid.spread_rows(ahead_column, owner)
            ahead_state = next(ahead_task)
        if before is None:
            reflect_cols, q_cols = reflect(panel_cols, coef, add, place_col)
            local = multiply(matrix, reflect_cols)
        else:
            last_q_rows, last_y_rows, last_q_cols, last_y_cols = before
            reflect_cols, q_cols, cross = reflect(
                panel_cols, coef, add, place_col, (last_y_cols, last_q_cols)
            )
            local = multiply(matrix, reflect_cols, (last_q_rows, last_y_rows, cross))
        reflect_rows, q_rows = reflect(panel_rows, coef, add, place_row)
        inner = matmul(reflect_rows, local, 0, 0)
        if last:
            tasks = [product_task(grid, local), inner_task(grid, inner)]
        else:
            local, *ahead_state = tie(local, *ahead_state)
            tasks = [
                product_task(grid, local),
                inner_task(grid, inner, raw_cols, reflect_cols),
                ahead_rows_task(grid, ahead_task, ahead_state),
            ]
        if before is not None:
            tasks.append(update_task(grid, matrix, before))
        results = lockstep(*tasks)
        product_rows, product_cols = results[0]
        inner = results[1]
        half_inner = 0.5 * inner[:, :B]
        if before is not None:
            matrix, product_cols = tie(results[-1], product_cols)
        if last:
            y_rows = companion(product_rows, q_rows, half_inner, 1)
            y_cols = companion(product_cols, q_cols, half_inner, fold)
        else:
            y_block = inner[:, B:] - matmul(q_block, half_inner, 1, 0)
            y_cols, panel_cols, square = companion(
                product_cols, q_cols, half_inner, fold,
                (raw_cols, y_block, q_block, grid.cols, panel + 1, grid.q, True),
            )
            next_q, next_col = block_of(panel + 2, grid.cols)
            top = (grid.q == next_q) * panel_cols[next_col : next_col + B]
            sums = jnp.concatenate((square, top), 1)
            half = B // 2
            sums = grid.halves(sums[:half], sums[half:])[0]
            y_rows, panel_rows = companion(
                product_rows, q_rows, half_inner, 1,
                (results[2], y_block, q_block, grid.rows, panel + 1, grid.p, False),
            )
            for bit in grid.col_bits:
                sums = sums + grid.swap(sums, 0, bit)
                sums, y_rows, panel_rows = tie(sums, y_rows, panel_rows)
            sums = grid.join_core(sums, grid.swap(sums, 1))
        before = (q_rows, y_rows, q_cols, y_cols)
    return update(matrix, *before)


def product_task(grid, local):
    parts = yield from grid.sum_scatter(local)
    piece = jnp.stack(parts).reshape(-1, local.shape[1])
    cols_task = grid.gather_cols(piece)
    (moved,) = yield next(cols_task)
    try:
        cols_task.send([moved])
    except StopIteration as stop:
        product_cols = stop.value
    product_rows = yield from grid.gather_rows(parts, local.shape[1])
    return product_rows, product_cols


def idle(stages):
    for _ in range(stages):
        yield []


def inner_task(grid, inner, raw_cols=None, reflect_cols=None):
    yield from idle(1)
    (inner,) = yield [grid.sum_core(inner)]
    for bit in grid.row_bits:
        (inner,) = yield [inner + grid.swap(inner, bit)]
    if raw_cols is not None:
        block = matmul(raw_cols, reflect_cols, 0, 0)
        half = B // 2
        inner = jnp.concatenate((inner, grid.halves(block[:half], block[half:])[0]), 1)
    for bit in grid.col_bits:
        (inner,) = yield [inner + grid.swap(inner, 0, bit)]
    (other,) = yield [grid.swap(inner, 1)]
    return grid.join_core(inner, other)


def ahead_rows_task(grid, task, state):
    yield from idle(1 + len(grid.row_bits) + len(grid.col_bits))
    state = yield state
    while True:
        try:
            state = task.send(state)
        except StopIteration as stop:
            return stop.value


def update_task(grid, matrix, before):
    yield from idle(len(grid.col_bits))
    (first,) = yield [before[0]]
    (half,) = yield [update(matrix, first, *before[1:], (0, 2))]
    return update(matrix, first, *before[1:], (1, 2), half)


def solution(mesh):
    return jax.shard_map(
        body,
        mesh=mesh,
        in_specs=(P("row", "col"),),
        out_specs=P("row", "col"),
        check_vma=False,
    )
```

```python
import functools
import jax
import jax.numpy as jnp
from jax import lax
from jax.experimental import pallas as pl
from jax.experimental.pallas import tpu as pltpu
from jax.sharding import PartitionSpec as P

B = 256
PANELS = 2
NS_STEPS = 12
INV_STEPS = 5
LEAF = 64
BOTH = ("row", "col")


HIGHEST = lax.Precision.HIGHEST
HIGH = lax.Precision.HIGH


def matmul(first_op, second_op, first_dim, second_dim, precision=HIGH):
    return lax.dot_general(
        first_op,
        second_op,
        (((first_dim,), (second_dim,)), ((), ())),
        precision=precision,
        preferred_element_type=jnp.float32,
    )


def split(value):
    high = value.astype(jnp.bfloat16)
    return high, (value - high.astype(jnp.float32)).astype(jnp.bfloat16)


def dot_split(first_op, second_op, first_dim, second_dim):
    (first_high, first_low), (second_high, second_low) = first_op, second_op
    return lax.dot_general(
        jnp.concatenate((first_high, first_high, first_low), first_dim),
        jnp.concatenate((second_high, second_low, second_high), second_dim),
        (((first_dim,), (second_dim,)), ((), ())),
        preferred_element_type=jnp.float32,
    )


def factor_kernel(gram_ref, top_ref, coef_ref, add_ref, block_ref, work):
    size = gram_ref.shape[0]
    lanes = 128
    row_id = lax.broadcasted_iota(jnp.int32, (size, size), 0)
    col_id = lax.broadcasted_iota(jnp.int32, (size, size), 1)
    eye = (row_id == col_id).astype(jnp.float32)
    work[:, :size] = gram_ref[...]
    work[:, size:] = eye
    leaf_row = lax.broadcasted_iota(jnp.int32, (LEAF, lanes), 0)
    leaf_lane = lax.broadcasted_iota(jnp.int32, (LEAF, lanes), 1)
    for start in range(0, size, LEAF):
        tile = start // lanes * lanes
        offset = start - tile
        part = work[start : start + LEAF, tile : tile + lanes]
        trace = (leaf_row == leaf_lane).astype(jnp.float32)
        for pivot in range(LEAF):
            lane = offset + pivot
            scale = 1.0 / part[pivot : pivot + 1, lane : lane + 1]
            column = jnp.where(leaf_row > pivot, part[:, lane : lane + 1], 0.0)
            part, trace = (
                part - column * (part[pivot : pivot + 1, :] * scale),
                trace - column * (trace[pivot : pivot + 1, :] * scale),
            )
        pivots = jnp.sum(jnp.where(leaf_lane == leaf_row + offset, part, 0.0), axis=1, keepdims=True)
        root = lax.rsqrt(pivots)
        root = root * (1.5 - 0.5 * pivots * root * root)
        leaf_inv = (trace * root)[:, :LEAF]
        low, high = tile, size + tile + lanes
        rows = matmul(leaf_inv, work[start : start + LEAF, low:high], 1, 0, HIGHEST)
        work[start : start + LEAF, low:high] = rows
        below = start + LEAF
        if below < size:
            below_tile = below // lanes * lanes
            change = matmul(rows[:, below_tile - low : size - low], rows, 0, 0, HIGHEST)
            work[below:, low:high] = work[below:, low:high] - change[below - below_tile :, :]
    inverse_low = work[:, size:]
    inverse_up = inverse_low.T
    top_basis = matmul(top_ref[...], inverse_up, 1, 0, HIGHEST)

    def polar_step(step, polar):
        parts = split(polar)
        square = dot_split(parts, parts, 0, 0)
        return 1.5 * polar - 0.5 * dot_split(parts, split(square), 1, 0)

    polar = lax.fori_loop(0, NS_STEPS, polar_step, top_basis)
    polar_parts = split(polar)
    cross = dot_split(polar_parts, split(top_basis), 0, 0)
    metric = eye + cross + cross.T + dot_split(polar_parts, polar_parts, 0, 0)
    metric_parts = split(metric)

    def inverse_step(step, guess):
        parts = split(guess)
        return 2.0 * guess - dot_split(parts, split(dot_split(metric_parts, parts, 1, 0)), 1, 0)

    guess = (40.0 / 41.0) * eye - (8.0 / 41.0) * metric
    middle = split(2.0 * lax.fori_loop(0, INV_STEPS, inverse_step, guess))
    coef_ref[:, :size] = inverse_up
    coef_ref[:, size:] = dot_split(split(inverse_up), middle, 1, 0)
    add_ref[:, :size] = polar
    add_ref[:, size:] = dot_split(polar_parts, middle, 1, 0)
    block_ref[...] = dot_split(split(top_basis + polar), middle, 1, 0)


def factors(gram, top):
    size = gram.shape[0]
    wide = jax.ShapeDtypeStruct((size, 2 * size), jnp.float32)
    return pl.pallas_call(
        factor_kernel,
        out_shape=(wide, wide, jax.ShapeDtypeStruct(gram.shape, jnp.float32)),
        scratch_shapes=[pltpu.VMEM((size, 2 * size), jnp.float32)],
        cost_estimate=pl.CostEstimate(flops=40_000_000_000, bytes_accessed=2_000_000, transcendentals=0),
        name="factors",
    )(gram, top)


def product_of(first_op, second_op, first_dim, second_dim):
    return dot_split(split(first_op), split(second_op), first_dim, second_dim)


def turn_kernel(stride, above, place, block_ref, out_ref):
    tile = block_ref[...].T
    index = pl.program_id(0) * tile.shape[0] + lax.broadcasted_iota(jnp.int32, tile.shape, 0)
    keep = (place[0] == 1) & (index // tile.shape[1] * stride + place[1] > above)
    out_ref[...] = jnp.where(keep, tile, 0.0)


def turn(matrix, row_block, keep, stride, rank, above):
    cols = matrix.shape[1]
    width = min(1024, cols)
    return pl.pallas_call(
        functools.partial(turn_kernel, stride, above),
        out_shape=jax.ShapeDtypeStruct((cols, B), jnp.float32),
        grid_spec=pltpu.PrefetchScalarGridSpec(
            num_scalar_prefetch=1,
            grid=(cols // width,),
            in_specs=[pl.BlockSpec((B, width), lambda i, place: (row_block, i))],
            out_specs=pl.BlockSpec((width, B), lambda i, place: (i, 0)),
        ),
        cost_estimate=pl.CostEstimate(flops=0, bytes_accessed=8 * cols * B, transcendentals=0),
        name="turn",
    )(jnp.stack((keep.astype(jnp.int32), rank.astype(jnp.int32))), matrix)


def reflect_kernel(place, panel_ref, coef_ref, add_ref, *refs):
    reflect_ref, scaled_ref = refs[-3:-1] if len(refs) > 2 else refs
    size = panel_ref.shape[1]
    step = pl.program_id(0)
    both = product_of(panel_ref[...], coef_ref[...], 1, 0)
    reflect_ref[...] = both[:, :size]
    scaled_ref[...] = both[:, size:]
    per = panel_ref.shape[0] // size
    inside = place[0] - step * per

    @pl.when((inside >= 0) & (inside < per))
    def _():
        rows = pl.ds(pl.multiple_of(jnp.clip(inside, 0, per - 1) * size, size), size)
        reflect_ref[rows, :] += add_ref[:, :size]
        scaled_ref[rows, :] += add_ref[:, size:]

    if len(refs) > 2:
        y_ref, q_ref, inner_ref = refs[0], refs[1], refs[-1]

        @pl.when(step == 0)
        def _():
            inner_ref[...] = jnp.zeros_like(inner_ref)

        parts = split(reflect_ref[...])
        inner_ref[:size, :] += dot_split(split(y_ref[...]), parts, 0, 0)
        inner_ref[size:, :] += dot_split(split(q_ref[...]), parts, 0, 0)


def reflect(panel, coef, add, place, before=()):
    size = coef.shape[0]
    rows = min(4 * size, panel.shape[0])
    block = pl.BlockSpec((rows, size), lambda i, place: (i, 0))
    fixed = pl.BlockSpec((size, 2 * size), lambda i, place: (0, 0))
    out = jax.ShapeDtypeStruct(panel.shape, jnp.float32)
    extra = [pl.BlockSpec((2 * size, size), lambda i, place: (0, 0))] if before else []
    return pl.pallas_call(
        reflect_kernel,
        out_shape=[out, out] + [jax.ShapeDtypeStruct((2 * size, size), jnp.float32) for _ in extra],
        grid_spec=pltpu.PrefetchScalarGridSpec(
            num_scalar_prefetch=1,
            grid=(panel.shape[0] // rows,),
            in_specs=[block, fixed, fixed] + [block for _ in before],
            out_specs=[block, block] + extra,
        ),
        cost_estimate=pl.CostEstimate(
            flops=12 * panel.size * size, bytes_accessed=12 * panel.size, transcendentals=0
        ),
        name="reflect",
    )(place.reshape(1), panel, coef, add, *before)


def multiply_kernel(matrix_ref, panel_ref, *refs):
    out_ref, stored = refs[-2:]
    cols = panel_ref.shape[0]
    depth = min(1024, cols)

    @pl.when(pl.program_id(0) == 0)
    def _():
        for start in range(0, cols, depth):
            high, low = split(panel_ref[start : start + depth, :])
            stored[3 * start : 3 * (start + depth), :] = jnp.concatenate((high, low, high), 0)

    total = None
    for start in range(0, cols, depth):
        high, low = split(matrix_ref[:, start : start + depth])
        part = jnp.dot(
            jnp.concatenate((high, high, low), 1),
            stored[3 * start : 3 * (start + depth), :],
            preferred_element_type=jnp.float32,
        )
        total = part if total is None else total + part
    if len(refs) > 2:
        q_ref, y_ref, inner_ref = refs[:3]
        both = jnp.concatenate((q_ref[...], y_ref[...]), 1)
        total = total - product_of(both, inner_ref[...], 1, 0)
    out_ref[...] = total


def multiply(matrix, panel, change=()):
    rows, cols = matrix.shape
    size = panel.shape[1]
    height = min(512, rows)
    side = pl.BlockSpec((height, size), lambda i: (i, 0))
    return pl.pallas_call(
        multiply_kernel,
        out_shape=jax.ShapeDtypeStruct((rows, size), jnp.float32),
        grid=(rows // height,),
        in_specs=[
            pl.BlockSpec((height, cols), lambda i: (i, 0)),
            pl.BlockSpec((cols, size), lambda i: (0, 0), pipeline_mode=pl.Buffered(1)),
        ]
        + ([side, side, pl.BlockSpec((2 * size, size), lambda i: (0, 0))] if change else []),
        out_specs=side,
        scratch_shapes=[pltpu.VMEM((3 * cols, size), jnp.bfloat16)],
        compiler_params=pltpu.CompilerParams(vmem_limit_bytes=60 << 20),
        cost_estimate=pl.CostEstimate(
            flops=6 * rows * cols * size, bytes_accessed=4 * matrix.size, transcendentals=0
        ),
        name="multiply",
    )(matrix, panel, *change)


def interleave(ref, size):
    parts, rows, _ = ref.shape
    if parts == 1:
        return ref[0]
    return jnp.concatenate(
        [
            ref[part, index * size : (index + 1) * size, :]
            for index in range(rows // size)
            for part in range(parts)
        ],
        0,
    )


def companion_kernel(product_ref, scaled_ref, inner_ref, out_ref):
    product = interleave(product_ref, inner_ref.shape[0])
    out_ref[...] = product - product_of(scaled_ref[...], inner_ref[...], 1, 0)


def next_kernel(
    stride, above, grams, rank, product_ref, scaled_ref, inner_ref, raw_ref, left_ref, right_ref, out_ref, next_ref, *gram
):
    size = inner_ref.shape[0]
    step = pl.program_id(0)
    scaled = split(scaled_ref[...])
    companion = interleave(product_ref, size) - dot_split(scaled, split(inner_ref[...]), 1, 0)
    out_ref[...] = companion
    change = dot_split(scaled, split(left_ref[...]), 1, 1) + product_of(companion, right_ref[...], 1, 1)
    index = step * companion.shape[0] + lax.broadcasted_iota(jnp.int32, companion.shape, 0)
    panel = jnp.where(index // size * stride + rank[0] > above, raw_ref[...] - change, 0.0)
    next_ref[...] = panel
    if grams:
        square = matmul(panel, panel, 0, 0, HIGHEST)

        @pl.when(step == 0)
        def _():
            gram[0][...] = square

        @pl.when(step > 0)
        def _():
            gram[0][...] += square


def companion(product, scaled, inner, fold, ahead=None):
    size = inner.shape[0]
    total = scaled.shape[0]
    each = total // fold
    rows = min(max(4 // fold, 1) * size, each)
    source = pl.BlockSpec((fold, rows, size), lambda i, *_: (0, i, 0))
    block = pl.BlockSpec((fold * rows, size), lambda i, *_: (i, 0))
    fixed = pl.BlockSpec((size, size), lambda i, *_: (0, 0))
    out = jax.ShapeDtypeStruct(scaled.shape, jnp.float32)
    product = product.reshape(fold, each, size)
    if ahead is None:
        return pl.pallas_call(
            companion_kernel,
            out_shape=out,
            grid=(each // rows,),
            in_specs=[source, block, fixed],
            out_specs=block,
            cost_estimate=pl.CostEstimate(
                flops=6 * scaled.size * size, bytes_accessed=12 * scaled.size, transcendentals=0
            ),
            name="companion",
        )(product, scaled, inner)
    raw, y_block, q_block, stride, above, rank, grams = ahead
    return pl.pallas_call(
        functools.partial(next_kernel, stride, above, grams),
        out_shape=(out, out) + ((jax.ShapeDtypeStruct((size, size), jnp.float32),) if grams else ()),
        grid_spec=pltpu.PrefetchScalarGridSpec(
            num_scalar_prefetch=1,
            grid=(each // rows,),
            in_specs=[source, block, fixed, block, fixed, fixed],
            out_specs=[block, block] + ([fixed] if grams else []),
        ),
        cost_estimate=pl.CostEstimate(
            flops=30 * scaled.size * size, bytes_accessed=20 * scaled.size, transcendentals=0
        ),
        name="companion_next",
    )(rank.reshape(1), product, scaled, inner, raw, y_block, q_block)


def update_kernel(matrix_ref, q_rows_ref, y_rows_ref, q_cols_ref, y_cols_ref, *refs):
    out_ref, right = refs[-2:]
    size = q_rows_ref.shape[1]
    cols = matrix_ref.shape[1]
    width = 2 * size

    @pl.when(pl.program_id(0) == 0)
    def _():
        def fill(index, carry):
            span = pl.ds(pl.multiple_of(index * width, width), width)
            high, low = split(jnp.concatenate((y_cols_ref[span, :], q_cols_ref[span, :]), 1).T)
            right[:, span] = jnp.concatenate((high, low, high), 0)
            return carry

        lax.fori_loop(0, cols // width, fill, 0)

    high, low = split(jnp.concatenate((q_rows_ref[...], y_rows_ref[...]), 1))
    left = jnp.concatenate((high, high, low), 1)

    for start in range(0, cols, width):
        change = jnp.dot(left, right[:, start : start + width], preferred_element_type=jnp.float32)
        out_ref[:, start : start + width] = matrix_ref[:, start : start + width] - change


def update(matrix, q_rows, y_rows, q_cols, y_cols, span=(0, 1), into=None):
    size = q_rows.shape[1]
    rows, cols = matrix.shape
    part, parts = span
    steps = rows // size // parts
    start = part * steps
    tile = pl.BlockSpec((size, cols), lambda i: (start + i, 0))
    side = pl.BlockSpec((size, size), lambda i: (start + i, 0))
    whole = pl.BlockSpec((cols, size), lambda i: (0, 0), pipeline_mode=pl.Buffered(1))
    extra = [] if into is None else [into]
    return pl.pallas_call(
        update_kernel,
        out_shape=jax.ShapeDtypeStruct(matrix.shape, jnp.float32),
        grid=(steps,),
        in_specs=[tile, side, side, whole, whole] + [pl.BlockSpec(memory_space=pl.ANY) for _ in extra],
        out_specs=tile,
        scratch_shapes=[pltpu.VMEM((6 * size, cols), jnp.bfloat16)],
        input_output_aliases={5: 0} if extra else {},
        compiler_params=pltpu.CompilerParams(vmem_limit_bytes=60 << 20),
        cost_estimate=pl.CostEstimate(
            flops=12 * rows * cols * size // parts,
            bytes_accessed=8 * matrix.size // parts,
            transcendentals=0,
        ),
        name="update",
    )(matrix, q_rows, y_rows, q_cols, y_cols, *extra)


def tie(*arrays):
    return lax.optimization_barrier(arrays)


def lockstep(*tasks):
    results = [None] * len(tasks)
    states = {}

    def advance(place, *state):
        task = tasks[place]
        try:
            if isinstance(task, tuple) and not state:
                states[place] = task[0].send(task[1])
            elif isinstance(task, tuple):
                states[place] = task[0].send(*state)
            else:
                states[place] = task.send(*state) if state else next(task)
        except StopIteration as stop:
            results[place] = stop.value
            states.pop(place, None)

    for place in range(len(tasks)):
        advance(place)
    while states:
        flat, tree = jax.tree.flatten(states)
        ended = jax.tree.unflatten(tree, tie(*flat)) if flat else dict(states)
        for place in list(ended):
            advance(place, ended[place])
    return results


class Grid:
    def __init__(self):
        self.rows = lax.axis_size("row")
        self.cols = lax.axis_size("col")
        self.p = lax.axis_index("row")
        self.q = lax.axis_index("col")
        self.first = self.p % 2 == 0
        self.row_bits = [1 << bit for bit in range(1, self.rows.bit_length() - 1)]
        self.col_bits = [1 << bit for bit in range(self.cols.bit_length() - 1)]

    def swap(self, array, row_bit=0, col_bit=0, only=None):
        pairs = [
            (p * self.cols + q, (p ^ row_bit) * self.cols + (q ^ col_bit))
            for p in range(self.rows)
            for q in range(self.cols)
            if only is None or only(p, q)
        ]
        return lax.ppermute(array, BOTH, pairs)

    def halves(self, low, high):
        return jnp.where(self.first, low, high), jnp.where(self.first, high, low)

    def sum_core(self, array):
        half = array.shape[0] // 2
        kept, sent = self.halves(array[:half], array[half:])
        return kept + self.swap(sent, 1)

    def join_core(self, kept, other):
        low, high = self.halves(kept, other)
        return jnp.concatenate((low, high), 0)

    def spread_rows(self, array, owner):
        bits = self.col_bits
        parts = jnp.split(array, len(bits), 0)
        spans = [{owner} for _ in parts]
        for stage in range(len(bits)):
            new = []
            for turn, part in enumerate(parts):
                bit = bits[(turn + stage) % len(bits)]
                span = spans[turn]
                got = self.swap(part, 0, bit, lambda p, q: q in span)
                fresh = {q ^ bit for q in span}
                is_fresh = functools.reduce(jnp.logical_or, [self.q == q for q in sorted(fresh)])
                new.append(jnp.where(is_fresh, got, part))
                spans[turn] = span | fresh
            parts = yield new
        return jnp.concatenate(parts, 0)

    def sum_scatter(self, array):
        bits = self.col_bits
        count = len(bits)
        whole = array.reshape(*(2,) * count, count, -1, array.shape[1])
        parts = [whole[(slice(None),) * count + (turn,)] for turn in range(count)]
        left = [list(bits[::-1])] * count
        for stage in range(count):
            new = []
            for turn, part in enumerate(parts):
                bit = bits[(turn + stage) % count]
                axis = left[turn].index(bit)
                left[turn] = [other for other in left[turn] if other != bit]
                is_high = (self.q & bit) != 0
                low, high = (lax.index_in_dim(part, side, axis, False) for side in (0, 1))
                got = self.swap(jnp.where(is_high, low, high), 0, bit)
                new.append(jnp.where(is_high, high, low) + got)
            parts = yield new
        return parts

    def gather_rows(self, parts, width):
        bits = self.col_bits
        count = len(bits)
        orders = [[bits[(turn + stage) % count] for stage in range(count)] for turn in range(count)]
        held = [[] for _ in parts]
        for stage in reversed(range(count)):
            new = []
            for turn, part in enumerate(parts):
                bit = orders[turn][stage]
                held[turn] = sorted(held[turn] + [bit], reverse=True)
                axis = held[turn].index(bit)
                got = self.swap(part, 0, bit)
                is_high = (self.q & bit) != 0
                low, high = jnp.where(is_high, got, part), jnp.where(is_high, part, got)
                new.append(jnp.stack((low, high), axis))
            parts = yield new
        return jnp.stack(parts, count).reshape(-1, width)

    def gather_cols(self, piece):
        pairs = [
            (p * self.cols + q, (p // self.cols * self.cols + q) * self.cols + p % self.cols)
            for p in range(self.rows)
            for q in range(self.cols)
        ]
        (moved,) = yield [lax.ppermute(piece, BOTH, pairs)]
        return lax.all_gather(moved, "row", tiled=True)


def block_of(index, count):
    return index % count, index // count * B


def body(affinity):
    grid = Grid()
    rows_here, cols_here = affinity.shape
    row_blocks = jnp.arange(rows_here, dtype=jnp.int32) // B * grid.rows + grid.p
    col_blocks = jnp.arange(cols_here, dtype=jnp.int32) // B * grid.cols + grid.q
    matrix = affinity

    def column_of(panel):
        owner, start = block_of(panel, grid.cols)
        return matrix[:, start : start + B], owner

    def row_of(panel, above):
        owner, start = block_of(panel, grid.rows)
        return turn(matrix, start // B, grid.p == owner, grid.cols, grid.q, above)

    top_p, top_row = block_of(1, grid.rows)
    owned, owner = column_of(0)
    owned, block = tie(owned, row_of(0, 0))
    panel_cols = lax.psum(block, "row")
    owned = jnp.where((row_blocks > 0)[:, None], owned, 0.0)
    mine = (grid.q == owner).astype(jnp.float32)
    square = mine * matmul(owned, owned, 0, 0, HIGHEST)
    top = mine * (grid.p == top_p) * owned[top_row : top_row + B]
    sums = grid.sum_core(jnp.concatenate((square, top), 1))
    ahead_block = row_of(1, -1)
    for bit in grid.row_bits:
        sums = sums + grid.swap(sums, bit)
        sums, ahead_block = tie(sums, ahead_block)
    rows_task = grid.spread_rows(owned, owner)
    sums, *state = tie(sums, *next(rows_task))
    for bit in grid.col_bits:
        sums = sums + grid.swap(sums, 0, bit)
    sums = grid.join_core(sums, grid.swap(sums, 1))
    sums, *state = tie(sums, *state)
    (panel_rows,) = lockstep((rows_task, state))

    fold = grid.rows // grid.cols
    before = None
    for panel in range(PANELS):
        last = panel + 1 == PANELS
        top_p, top_row = block_of(panel + 1, grid.rows)
        top_q, top_col = block_of(panel + 1, grid.cols)
        coef, add, q_block = factors(sums[:, :B], sums[:, B:])
        place_row = jnp.where(grid.p == top_p, top_row // B, -1)
        place_col = jnp.where(grid.q == top_q, top_col // B, -1)
        if not last:
            ahead_column, owner = column_of(panel + 1)
            ahead_block, ahead_column, panel_cols, coef = tie(
                ahead_block, ahead_column, panel_cols, coef
            )
            raw_cols = lax.psum(ahead_block, "row")
            ahead_task = grid.spread_rows(ahead_column, owner)
            ahead_state = next(ahead_task)
        if before is None:
            reflect_cols, q_cols = reflect(panel_cols, coef, add, place_col)
            local = multiply(matrix, reflect_cols)
        else:
            last_q_rows, last_y_rows, last_q_cols, last_y_cols = before
            reflect_cols, q_cols, cross = reflect(
                panel_cols, coef, add, place_col, (last_y_cols, last_q_cols)
            )
            local = multiply(matrix, reflect_cols, (last_q_rows, last_y_rows, cross))
        reflect_rows, q_rows = reflect(panel_rows, coef, add, place_row)
        inner = matmul(reflect_rows, local, 0, 0)
        if last:
            tasks = [product_task(grid, local), inner_task(grid, inner)]
        else:
            local, *ahead_state = tie(local, *ahead_state)
            tasks = [
                product_task(grid, local),
                inner_task(grid, inner, raw_cols, reflect_cols),
                ahead_rows_task(grid, ahead_task, ahead_state),
            ]
        if before is not None:
            tasks.append(update_task(grid, matrix, before))
        results = lockstep(*tasks)
        product_rows, product_cols = results[0]
        inner = results[1]
        half_inner = 0.5 * inner[:, :B]
        if before is not None:
            matrix, product_cols = tie(results[-1], product_cols)
        if last:
            y_rows = companion(product_rows, q_rows, half_inner, 1)
            y_cols = companion(product_cols, q_cols, half_inner, fold)
        else:
            y_block = inner[:, B:] - matmul(q_block, half_inner, 1, 0)
            y_cols, panel_cols, square = companion(
                product_cols, q_cols, half_inner, fold,
                (raw_cols, y_block, q_block, grid.cols, panel + 1, grid.q, True),
            )
            next_q, next_col = block_of(panel + 2, grid.cols)
            top = (grid.q == next_q) * panel_cols[next_col : next_col + B]
            sums = jnp.concatenate((square, top), 1)
            half = B // 2
            sums = grid.halves(sums[:half], sums[half:])[0]
            y_rows, panel_rows = companion(
                product_rows, q_rows, half_inner, 1,
                (results[2], y_block, q_block, grid.rows, panel + 1, grid.p, False),
            )
            for bit in grid.col_bits:
                sums = sums + grid.swap(sums, 0, bit)
                sums, y_rows, panel_rows = tie(sums, y_rows, panel_rows)
            sums = grid.join_core(sums, grid.swap(sums, 1))
        before = (q_rows, y_rows, q_cols, y_cols)
    return update(matrix, *before)


def product_task(grid, local):
    parts = yield from grid.sum_scatter(local)
    piece = jnp.stack(parts).reshape(-1, local.shape[1])
    cols_task = grid.gather_cols(piece)
    (moved,) = yield next(cols_task)
    try:
        cols_task.send([moved])
    except StopIteration as stop:
        product_cols = stop.value
    product_rows = yield from grid.gather_rows(parts, local.shape[1])
    return product_rows, product_cols


def idle(stages):
    for _ in range(stages):
        yield []


def inner_task(grid, inner, raw_cols=None, reflect_cols=None):
    yield from idle(1)
    (inner,) = yield [grid.sum_core(inner)]
    for bit in grid.row_bits:
        (inner,) = yield [inner + grid.swap(inner, bit)]
    if raw_cols is not None:
        block = matmul(raw_cols, reflect_cols, 0, 0)
        half = B // 2
        inner = jnp.concatenate((inner, grid.halves(block[:half], block[half:])[0]), 1)
    for bit in grid.col_bits:
        (inner,) = yield [inner + grid.swap(inner, 0, bit)]
    (other,) = yield [grid.swap(inner, 1)]
    return grid.join_core(inner, other)


def ahead_rows_task(grid, task, state):
    yield from idle(len(grid.col_bits) - 1)
    state = yield state
    while True:
        try:
            state = task.send(state)
        except StopIteration as stop:
            return stop.value
        yield from idle(1)
        state = yield state


def update_task(grid, matrix, before):
    yield from idle(len(grid.col_bits))
    (first,) = yield [before[0]]
    (half,) = yield [update(matrix, first, *before[1:], (0, 2))]
    (whole,) = yield [update(matrix, first, *before[1:], (1, 2), half)]
    return whole


def solution(mesh):
    return jax.shard_map(
        body,
        mesh=mesh,
        in_specs=(P("row", "col"),),
        out_specs=P("row", "col"),
        check_vma=False,
    )
```

```python
import functools
import jax
import jax.numpy as jnp
from jax import lax
from jax.experimental import pallas as pl
from jax.experimental.pallas import tpu as pltpu
from jax.sharding import PartitionSpec as P

B = 256
PANELS = 2
NS_STEPS = 12
INV_STEPS = 5
LEAF = 64
BOTH = ("row", "col")


HIGHEST = lax.Precision.HIGHEST
HIGH = lax.Precision.HIGH


def matmul(first_op, second_op, first_dim, second_dim, precision=HIGH):
    return lax.dot_general(
        first_op,
        second_op,
        (((first_dim,), (second_dim,)), ((), ())),
        precision=precision,
        preferred_element_type=jnp.float32,
    )


def split(value):
    high = value.astype(jnp.bfloat16)
    return high, (value - high.astype(jnp.float32)).astype(jnp.bfloat16)


def dot_split(first_op, second_op, first_dim, second_dim):
    (first_high, first_low), (second_high, second_low) = first_op, second_op
    return lax.dot_general(
        jnp.concatenate((first_high, first_high, first_low), first_dim),
        jnp.concatenate((second_high, second_low, second_high), second_dim),
        (((first_dim,), (second_dim,)), ((), ())),
        preferred_element_type=jnp.float32,
    )


def factor_kernel(gram_ref, top_ref, coef_ref, add_ref, block_ref, work):
    size = gram_ref.shape[0]
    lanes = 128
    row_id = lax.broadcasted_iota(jnp.int32, (size, size), 0)
    col_id = lax.broadcasted_iota(jnp.int32, (size, size), 1)
    eye = (row_id == col_id).astype(jnp.float32)
    work[:, :size] = gram_ref[...]
    work[:, size:] = eye
    leaf_row = lax.broadcasted_iota(jnp.int32, (LEAF, lanes), 0)
    leaf_lane = lax.broadcasted_iota(jnp.int32, (LEAF, lanes), 1)
    for start in range(0, size, LEAF):
        tile = start // lanes * lanes
        offset = start - tile
        part = work[start : start + LEAF, tile : tile + lanes]
        trace = (leaf_row == leaf_lane).astype(jnp.float32)
        for pivot in range(LEAF):
            lane = offset + pivot
            scale = 1.0 / part[pivot : pivot + 1, lane : lane + 1]
            column = jnp.where(leaf_row > pivot, part[:, lane : lane + 1], 0.0)
            part, trace = (
                part - column * (part[pivot : pivot + 1, :] * scale),
                trace - column * (trace[pivot : pivot + 1, :] * scale),
            )
        pivots = jnp.sum(jnp.where(leaf_lane == leaf_row + offset, part, 0.0), axis=1, keepdims=True)
        root = lax.rsqrt(pivots)
        root = root * (1.5 - 0.5 * pivots * root * root)
        leaf_inv = (trace * root)[:, :LEAF]
        low, high = tile, size + tile + lanes
        rows = matmul(leaf_inv, work[start : start + LEAF, low:high], 1, 0, HIGHEST)
        work[start : start + LEAF, low:high] = rows
        below = start + LEAF
        if below < size:
            below_tile = below // lanes * lanes
            change = matmul(rows[:, below_tile - low : size - low], rows, 0, 0, HIGHEST)
            work[below:, low:high] = work[below:, low:high] - change[below - below_tile :, :]
    inverse_low = work[:, size:]
    inverse_up = inverse_low.T
    top_basis = matmul(top_ref[...], inverse_up, 1, 0, HIGHEST)

    def polar_step(step, polar):
        parts = split(polar)
        square = dot_split(parts, parts, 0, 0)
        return 1.5 * polar - 0.5 * dot_split(parts, split(square), 1, 0)

    polar = lax.fori_loop(0, NS_STEPS, polar_step, top_basis)
    polar_parts = split(polar)
    cross = dot_split(polar_parts, split(top_basis), 0, 0)
    metric = eye + cross + cross.T + dot_split(polar_parts, polar_parts, 0, 0)
    metric_parts = split(metric)

    def inverse_step(step, guess):
        parts = split(guess)
        return 2.0 * guess - dot_split(parts, split(dot_split(metric_parts, parts, 1, 0)), 1, 0)

    guess = (40.0 / 41.0) * eye - (8.0 / 41.0) * metric
    middle = split(2.0 * lax.fori_loop(0, INV_STEPS, inverse_step, guess))
    coef_ref[:, :size] = inverse_up
    coef_ref[:, size:] = dot_split(split(inverse_up), middle, 1, 0)
    add_ref[:, :size] = polar
    add_ref[:, size:] = dot_split(polar_parts, middle, 1, 0)
    block_ref[...] = dot_split(split(top_basis + polar), middle, 1, 0)


def factors(gram, top):
    size = gram.shape[0]
    wide = jax.ShapeDtypeStruct((size, 2 * size), jnp.float32)
    return pl.pallas_call(
        factor_kernel,
        out_shape=(wide, wide, jax.ShapeDtypeStruct(gram.shape, jnp.float32)),
        scratch_shapes=[pltpu.VMEM((size, 2 * size), jnp.float32)],
        cost_estimate=pl.CostEstimate(flops=40_000_000_000, bytes_accessed=2_000_000, transcendentals=0),
        name="factors",
    )(gram, top)


def product_of(first_op, second_op, first_dim, second_dim):
    return dot_split(split(first_op), split(second_op), first_dim, second_dim)


def turn_kernel(stride, above, place, block_ref, out_ref):
    tile = block_ref[...].T
    index = pl.program_id(0) * tile.shape[0] + lax.broadcasted_iota(jnp.int32, tile.shape, 0)
    keep = (place[0] == 1) & (index // tile.shape[1] * stride + place[1] > above)
    out_ref[...] = jnp.where(keep, tile, 0.0)


def turn(matrix, row_block, keep, stride, rank, above):
    cols = matrix.shape[1]
    width = min(1024, cols)
    return pl.pallas_call(
        functools.partial(turn_kernel, stride, above),
        out_shape=jax.ShapeDtypeStruct((cols, B), jnp.float32),
        grid_spec=pltpu.PrefetchScalarGridSpec(
            num_scalar_prefetch=1,
            grid=(cols // width,),
            in_specs=[pl.BlockSpec((B, width), lambda i, place: (row_block, i))],
            out_specs=pl.BlockSpec((width, B), lambda i, place: (i, 0)),
        ),
        cost_estimate=pl.CostEstimate(flops=0, bytes_accessed=8 * cols * B, transcendentals=0),
        name="turn",
    )(jnp.stack((keep.astype(jnp.int32), rank.astype(jnp.int32))), matrix)


def reflect_kernel(place, panel_ref, coef_ref, add_ref, *refs):
    reflect_ref, scaled_ref = refs[-3:-1] if len(refs) > 2 else refs
    size = panel_ref.shape[1]
    step = pl.program_id(0)
    both = product_of(panel_ref[...], coef_ref[...], 1, 0)
    reflect_ref[...] = both[:, :size]
    scaled_ref[...] = both[:, size:]
    per = panel_ref.shape[0] // size
    inside = place[0] - step * per

    @pl.when((inside >= 0) & (inside < per))
    def _():
        rows = pl.ds(pl.multiple_of(jnp.clip(inside, 0, per - 1) * size, size), size)
        reflect_ref[rows, :] += add_ref[:, :size]
        scaled_ref[rows, :] += add_ref[:, size:]

    if len(refs) > 2:
        y_ref, q_ref, inner_ref = refs[0], refs[1], refs[-1]

        @pl.when(step == 0)
        def _():
            inner_ref[...] = jnp.zeros_like(inner_ref)

        parts = split(reflect_ref[...])
        inner_ref[:size, :] += dot_split(split(y_ref[...]), parts, 0, 0)
        inner_ref[size:, :] += dot_split(split(q_ref[...]), parts, 0, 0)


def reflect(panel, coef, add, place, before=()):
    size = coef.shape[0]
    rows = min(4 * size, panel.shape[0])
    block = pl.BlockSpec((rows, size), lambda i, place: (i, 0))
    fixed = pl.BlockSpec((size, 2 * size), lambda i, place: (0, 0))
    out = jax.ShapeDtypeStruct(panel.shape, jnp.float32)
    extra = [pl.BlockSpec((2 * size, size), lambda i, place: (0, 0))] if before else []
    return pl.pallas_call(
        reflect_kernel,
        out_shape=[out, out] + [jax.ShapeDtypeStruct((2 * size, size), jnp.float32) for _ in extra],
        grid_spec=pltpu.PrefetchScalarGridSpec(
            num_scalar_prefetch=1,
            grid=(panel.shape[0] // rows,),
            in_specs=[block, fixed, fixed] + [block for _ in before],
            out_specs=[block, block] + extra,
        ),
        cost_estimate=pl.CostEstimate(
            flops=12 * panel.size * size, bytes_accessed=12 * panel.size, transcendentals=0
        ),
        name="reflect",
    )(place.reshape(1), panel, coef, add, *before)


def multiply_kernel(matrix_ref, panel_ref, *refs):
    out_ref, stored = refs[-2:]
    cols = panel_ref.shape[0]
    depth = min(1024, cols)

    @pl.when(pl.program_id(0) == 0)
    def _():
        for start in range(0, cols, depth):
            high, low = split(panel_ref[start : start + depth, :])
            stored[3 * start : 3 * (start + depth), :] = jnp.concatenate((high, low, high), 0)

    total = None
    for start in range(0, cols, depth):
        high, low = split(matrix_ref[:, start : start + depth])
        part = jnp.dot(
            jnp.concatenate((high, high, low), 1),
            stored[3 * start : 3 * (start + depth), :],
            preferred_element_type=jnp.float32,
        )
        total = part if total is None else total + part
    if len(refs) > 2:
        q_ref, y_ref, inner_ref = refs[:3]
        both = jnp.concatenate((q_ref[...], y_ref[...]), 1)
        total = total - product_of(both, inner_ref[...], 1, 0)
    out_ref[...] = total


def multiply(matrix, panel, change=()):
    rows, cols = matrix.shape
    size = panel.shape[1]
    height = min(512, rows)
    side = pl.BlockSpec((height, size), lambda i: (i, 0))
    return pl.pallas_call(
        multiply_kernel,
        out_shape=jax.ShapeDtypeStruct((rows, size), jnp.float32),
        grid=(rows // height,),
        in_specs=[
            pl.BlockSpec((height, cols), lambda i: (i, 0)),
            pl.BlockSpec((cols, size), lambda i: (0, 0), pipeline_mode=pl.Buffered(1)),
        ]
        + ([side, side, pl.BlockSpec((2 * size, size), lambda i: (0, 0))] if change else []),
        out_specs=side,
        scratch_shapes=[pltpu.VMEM((3 * cols, size), jnp.bfloat16)],
        compiler_params=pltpu.CompilerParams(vmem_limit_bytes=60 << 20),
        cost_estimate=pl.CostEstimate(
            flops=6 * rows * cols * size, bytes_accessed=4 * matrix.size, transcendentals=0
        ),
        name="multiply",
    )(matrix, panel, *change)


def interleave(ref, size):
    parts, rows, _ = ref.shape
    if parts == 1:
        return ref[0]
    return jnp.concatenate(
        [
            ref[part, index * size : (index + 1) * size, :]
            for index in range(rows // size)
            for part in range(parts)
        ],
        0,
    )


def companion_kernel(product_ref, scaled_ref, inner_ref, out_ref):
    product = interleave(product_ref, inner_ref.shape[0])
    out_ref[...] = product - product_of(scaled_ref[...], inner_ref[...], 1, 0)


def next_kernel(
    stride, above, grams, rank, product_ref, scaled_ref, inner_ref, raw_ref, left_ref, right_ref, out_ref, next_ref, *gram
):
    size = inner_ref.shape[0]
    step = pl.program_id(0)
    scaled = split(scaled_ref[...])
    companion = interleave(product_ref, size) - dot_split(scaled, split(inner_ref[...]), 1, 0)
    out_ref[...] = companion
    change = dot_split(scaled, split(left_ref[...]), 1, 1) + product_of(companion, right_ref[...], 1, 1)
    index = step * companion.shape[0] + lax.broadcasted_iota(jnp.int32, companion.shape, 0)
    panel = jnp.where(index // size * stride + rank[0] > above, raw_ref[...] - change, 0.0)
    next_ref[...] = panel
    if grams:
        square = matmul(panel, panel, 0, 0, HIGHEST)

        @pl.when(step == 0)
        def _():
            gram[0][...] = square

        @pl.when(step > 0)
        def _():
            gram[0][...] += square


def companion(product, scaled, inner, fold, ahead=None):
    size = inner.shape[0]
    total = scaled.shape[0]
    each = total // fold
    rows = min(max(4 // fold, 1) * size, each)
    source = pl.BlockSpec((fold, rows, size), lambda i, *_: (0, i, 0))
    block = pl.BlockSpec((fold * rows, size), lambda i, *_: (i, 0))
    fixed = pl.BlockSpec((size, size), lambda i, *_: (0, 0))
    out = jax.ShapeDtypeStruct(scaled.shape, jnp.float32)
    product = product.reshape(fold, each, size)
    if ahead is None:
        return pl.pallas_call(
            companion_kernel,
            out_shape=out,
            grid=(each // rows,),
            in_specs=[source, block, fixed],
            out_specs=block,
            cost_estimate=pl.CostEstimate(
                flops=6 * scaled.size * size, bytes_accessed=12 * scaled.size, transcendentals=0
            ),
            name="companion",
        )(product, scaled, inner)
    raw, y_block, q_block, stride, above, rank, grams = ahead
    return pl.pallas_call(
        functools.partial(next_kernel, stride, above, grams),
        out_shape=(out, out) + ((jax.ShapeDtypeStruct((size, size), jnp.float32),) if grams else ()),
        grid_spec=pltpu.PrefetchScalarGridSpec(
            num_scalar_prefetch=1,
            grid=(each // rows,),
            in_specs=[source, block, fixed, block, fixed, fixed],
            out_specs=[block, block] + ([fixed] if grams else []),
        ),
        cost_estimate=pl.CostEstimate(
            flops=30 * scaled.size * size, bytes_accessed=20 * scaled.size, transcendentals=0
        ),
        name="companion_next",
    )(rank.reshape(1), product, scaled, inner, raw, y_block, q_block)


def update_kernel(matrix_ref, q_rows_ref, y_rows_ref, q_cols_ref, y_cols_ref, *refs):
    out_ref, right = refs[-2:]
    size = q_rows_ref.shape[1]
    cols = matrix_ref.shape[1]
    width = 2 * size

    @pl.when(pl.program_id(0) == 0)
    def _():
        def fill(index, carry):
            span = pl.ds(pl.multiple_of(index * width, width), width)
            high, low = split(jnp.concatenate((y_cols_ref[span, :], q_cols_ref[span, :]), 1).T)
            right[:, span] = jnp.concatenate((high, low, high), 0)
            return carry

        lax.fori_loop(0, cols // width, fill, 0)

    high, low = split(jnp.concatenate((q_rows_ref[...], y_rows_ref[...]), 1))
    left = jnp.concatenate((high, high, low), 1)

    for start in range(0, cols, width):
        change = jnp.dot(left, right[:, start : start + width], preferred_element_type=jnp.float32)
        out_ref[:, start : start + width] = matrix_ref[:, start : start + width] - change


def update(matrix, q_rows, y_rows, q_cols, y_cols, span=(0, 1), into=None):
    size = q_rows.shape[1]
    rows, cols = matrix.shape
    part, parts = span
    steps = rows // size // parts
    start = part * steps
    tile = pl.BlockSpec((size, cols), lambda i: (start + i, 0))
    side = pl.BlockSpec((size, size), lambda i: (start + i, 0))
    whole = pl.BlockSpec((cols, size), lambda i: (0, 0), pipeline_mode=pl.Buffered(1))
    extra = [] if into is None else [into]
    return pl.pallas_call(
        update_kernel,
        out_shape=jax.ShapeDtypeStruct(matrix.shape, jnp.float32),
        grid=(steps,),
        in_specs=[tile, side, side, whole, whole] + [pl.BlockSpec(memory_space=pl.ANY) for _ in extra],
        out_specs=tile,
        scratch_shapes=[pltpu.VMEM((6 * size, cols), jnp.bfloat16)],
        input_output_aliases={5: 0} if extra else {},
        compiler_params=pltpu.CompilerParams(vmem_limit_bytes=60 << 20),
        cost_estimate=pl.CostEstimate(
            flops=12 * rows * cols * size // parts,
            bytes_accessed=8 * matrix.size // parts,
            transcendentals=0,
        ),
        name="update",
    )(matrix, q_rows, y_rows, q_cols, y_cols, *extra)


def tie(*arrays):
    return lax.optimization_barrier(arrays)


def lockstep(*tasks):
    results = [None] * len(tasks)
    states = {}

    def advance(place, *state):
        task = tasks[place]
        try:
            if isinstance(task, tuple) and not state:
                states[place] = task[0].send(task[1])
            elif isinstance(task, tuple):
                states[place] = task[0].send(*state)
            else:
                states[place] = task.send(*state) if state else next(task)
        except StopIteration as stop:
            results[place] = stop.value
            states.pop(place, None)

    for place in range(len(tasks)):
        advance(place)
    while states:
        flat, tree = jax.tree.flatten(states)
        ended = jax.tree.unflatten(tree, tie(*flat)) if flat else dict(states)
        for place in list(ended):
            advance(place, ended[place])
    return results


class Grid:
    def __init__(self):
        self.rows = lax.axis_size("row")
        self.cols = lax.axis_size("col")
        self.p = lax.axis_index("row")
        self.q = lax.axis_index("col")
        self.first = self.p % 2 == 0
        self.row_bits = [1 << bit for bit in range(1, self.rows.bit_length() - 1)]
        self.col_bits = [1 << bit for bit in range(self.cols.bit_length() - 1)]

    def swap(self, array, row_bit=0, col_bit=0, only=None):
        pairs = [
            (p * self.cols + q, (p ^ row_bit) * self.cols + (q ^ col_bit))
            for p in range(self.rows)
            for q in range(self.cols)
            if only is None or only(p, q)
        ]
        return lax.ppermute(array, BOTH, pairs)

    def halves(self, low, high):
        return jnp.where(self.first, low, high), jnp.where(self.first, high, low)

    def sum_core(self, array):
        half = array.shape[0] // 2
        kept, sent = self.halves(array[:half], array[half:])
        return kept + self.swap(sent, 1)

    def join_core(self, kept, other):
        low, high = self.halves(kept, other)
        return jnp.concatenate((low, high), 0)

    def spread_rows(self, array, owner):
        bits = self.col_bits
        parts = jnp.split(array, len(bits), 0)
        spans = [{owner} for _ in parts]
        for stage in range(len(bits)):
            new = []
            for turn, part in enumerate(parts):
                bit = bits[(turn + stage) % len(bits)]
                span = spans[turn]
                got = self.swap(part, 0, bit, lambda p, q: q in span)
                fresh = {q ^ bit for q in span}
                is_fresh = functools.reduce(jnp.logical_or, [self.q == q for q in sorted(fresh)])
                new.append(jnp.where(is_fresh, got, part))
                spans[turn] = span | fresh
            parts = yield new
        return jnp.concatenate(parts, 0)

    def sum_scatter(self, array):
        bits = self.col_bits
        count = len(bits)
        whole = array.reshape(*(2,) * count, count, -1, array.shape[1])
        parts = [whole[(slice(None),) * count + (turn,)] for turn in range(count)]
        left = [list(bits[::-1])] * count
        for stage in range(count):
            new = []
            for turn, part in enumerate(parts):
                bit = bits[(turn + stage) % count]
                axis = left[turn].index(bit)
                left[turn] = [other for other in left[turn] if other != bit]
                is_high = (self.q & bit) != 0
                low, high = (lax.index_in_dim(part, side, axis, False) for side in (0, 1))
                got = self.swap(jnp.where(is_high, low, high), 0, bit)
                new.append(jnp.where(is_high, high, low) + got)
            parts = yield new
        return parts

    def gather_rows(self, parts, width):
        bits = self.col_bits
        count = len(bits)
        orders = [[bits[(turn + stage) % count] for stage in range(count)] for turn in range(count)]
        held = [[] for _ in parts]
        for stage in reversed(range(count)):
            new = []
            for turn, part in enumerate(parts):
                bit = orders[turn][stage]
                held[turn] = sorted(held[turn] + [bit], reverse=True)
                axis = held[turn].index(bit)
                got = self.swap(part, 0, bit)
                is_high = (self.q & bit) != 0
                low, high = jnp.where(is_high, got, part), jnp.where(is_high, part, got)
                new.append(jnp.stack((low, high), axis))
            parts = yield new
        return jnp.stack(parts, count).reshape(-1, width)

    def gather_cols(self, piece):
        pairs = [
            (p * self.cols + q, (p // self.cols * self.cols + q) * self.cols + p % self.cols)
            for p in range(self.rows)
            for q in range(self.cols)
        ]
        (moved,) = yield [lax.ppermute(piece, BOTH, pairs)]
        return lax.all_gather(moved, "row", tiled=True)


def block_of(index, count):
    return index % count, index // count * B


def body(affinity):
    grid = Grid()
    rows_here, cols_here = affinity.shape
    row_blocks = jnp.arange(rows_here, dtype=jnp.int32) // B * grid.rows + grid.p
    col_blocks = jnp.arange(cols_here, dtype=jnp.int32) // B * grid.cols + grid.q
    matrix = affinity

    def column_of(panel):
        owner, start = block_of(panel, grid.cols)
        return matrix[:, start : start + B], owner

    def row_of(panel, above):
        owner, start = block_of(panel, grid.rows)
        return turn(matrix, start // B, grid.p == owner, grid.cols, grid.q, above)

    top_p, top_row = block_of(1, grid.rows)
    owned, owner = column_of(0)
    owned, block = tie(owned, row_of(0, 0))
    panel_cols = lax.psum(block, "row")
    owned = jnp.where((row_blocks > 0)[:, None], owned, 0.0)
    mine = (grid.q == owner).astype(jnp.float32)
    square = mine * matmul(owned, owned, 0, 0, HIGHEST)
    top = mine * (grid.p == top_p) * owned[top_row : top_row + B]
    sums = grid.sum_core(jnp.concatenate((square, top), 1))
    ahead_block = row_of(1, -1)
    for bit in grid.row_bits:
        sums = sums + grid.swap(sums, bit)
        sums, ahead_block = tie(sums, ahead_block)
    rows_task = grid.spread_rows(owned, owner)
    sums, *state = tie(sums, *next(rows_task))
    for bit in grid.col_bits:
        sums = sums + grid.swap(sums, 0, bit)
    sums = grid.join_core(sums, grid.swap(sums, 1))
    sums, *state = tie(sums, *state)
    (panel_rows,) = lockstep((rows_task, state))

    fold = grid.rows // grid.cols
    before = None
    for panel in range(PANELS):
        last = panel + 1 == PANELS
        top_p, top_row = block_of(panel + 1, grid.rows)
        top_q, top_col = block_of(panel + 1, grid.cols)
        coef, add, q_block = factors(sums[:, :B], sums[:, B:])
        place_row = jnp.where(grid.p == top_p, top_row // B, -1)
        place_col = jnp.where(grid.q == top_q, top_col // B, -1)
        if not last:
            ahead_column, owner = column_of(panel + 1)
            ahead_block, ahead_column, panel_cols, coef = tie(
                ahead_block, ahead_column, panel_cols, coef
            )
            raw_cols = lax.psum(ahead_block, "row")
            ahead_task = grid.spread_rows(ahead_column, owner)
            ahead_state = next(ahead_task)
        if before is None:
            reflect_cols, q_cols = reflect(panel_cols, coef, add, place_col)
            local = multiply(matrix, reflect_cols)
        else:
            last_q_rows, last_y_rows, last_q_cols, last_y_cols = before
            reflect_cols, q_cols, cross = reflect(
                panel_cols, coef, add, place_col, (last_y_cols, last_q_cols)
            )
            local = multiply(matrix, reflect_cols, (last_q_rows, last_y_rows, cross))
        reflect_rows, q_rows = reflect(panel_rows, coef, add, place_row)
        inner = matmul(reflect_rows, local, 0, 0)
        if last:
            tasks = [product_task(grid, local), inner_task(grid, inner)]
        else:
            local, *ahead_state = tie(local, *ahead_state)
            tasks = [product_task(grid, local), inner_task(grid, inner, raw_cols, reflect_cols)]
        if before is not None:
            tasks.append(update_task(grid, matrix, before))
        results = lockstep(*tasks)
        product_rows, product_cols = results[0]
        inner = results[1]
        half_inner = 0.5 * inner[:, :B]
        if before is not None:
            matrix, product_cols = tie(results[-1], product_cols)
        if last:
            y_rows = companion(product_rows, q_rows, half_inner, 1)
            y_cols = companion(product_cols, q_cols, half_inner, fold)
        else:
            y_block = inner[:, B:] - matmul(q_block, half_inner, 1, 0)
            y_block, product_cols, *ahead_state = tie(y_block, product_cols, *ahead_state)
            (raw_rows,) = lockstep((ahead_task, ahead_state))
            y_cols, panel_cols, square = companion(
                product_cols, q_cols, half_inner, fold,
                (raw_cols, y_block, q_block, grid.cols, panel + 1, grid.q, True),
            )
            next_q, next_col = block_of(panel + 2, grid.cols)
            top = (grid.q == next_q) * panel_cols[next_col : next_col + B]
            sums = jnp.concatenate((square, top), 1)
            half = B // 2
            sums = grid.halves(sums[:half], sums[half:])[0]
            y_rows, panel_rows = companion(
                product_rows, q_rows, half_inner, 1,
                (raw_rows, y_block, q_block, grid.rows, panel + 1, grid.p, False),
            )
            for bit in grid.col_bits:
                sums = sums + grid.swap(sums, 0, bit)
            sums, y_rows, panel_rows = tie(sums, y_rows, panel_rows)
            sums = grid.join_core(sums, grid.swap(sums, 1))
        before = (q_rows, y_rows, q_cols, y_cols)
    return update(matrix, *before)


def product_task(grid, local):
    parts = yield from grid.sum_scatter(local)
    piece = jnp.stack(parts).reshape(-1, local.shape[1])
    cols_task = grid.gather_cols(piece)
    (moved,) = yield next(cols_task)
    try:
        cols_task.send([moved])
    except StopIteration as stop:
        product_cols = stop.value
    product_rows = yield from grid.gather_rows(parts, local.shape[1])
    return product_rows, product_cols


def idle(stages):
    for _ in range(stages):
        yield []


def inner_task(grid, inner, raw_cols=None, reflect_cols=None):
    yield from idle(1)
    (inner,) = yield [grid.sum_core(inner)]
    for bit in grid.row_bits[:-1]:
        (inner,) = yield [inner + grid.swap(inner, bit)]
    state = [inner + grid.swap(inner, grid.row_bits[-1])]
    if raw_cols is None:
        (inner,) = yield state
    else:
        inner, block = yield state + [matmul(raw_cols, reflect_cols, 0, 0)]
        half = B // 2
        inner = jnp.concatenate((inner, grid.halves(block[:half], block[half:])[0]), 1)
    for bit in grid.col_bits:
        (inner,) = yield [inner + grid.swap(inner, 0, bit)]
    (other,) = yield [grid.swap(inner, 1)]
    return grid.join_core(inner, other)


def update_task(grid, matrix, before):
    yield from idle(len(grid.col_bits))
    (first,) = yield [before[0]]
    (half,) = yield [update(matrix, first, *before[1:], (0, 2))]
    (whole,) = yield [update(matrix, first, *before[1:], (1, 2), half)]
    return whole


def solution(mesh):
    return jax.shard_map(
        body,
        mesh=mesh,
        in_specs=(P("row", "col"),),
        out_specs=P("row", "col"),
        check_vma=False,
    )
```
